32 devices in a mesh: dp: 8 (over z, y), tp: 4 (over x, core).
Axes of the slice: x: 2, y: 2, z: 4, core: 2. Of those that a mesh axis runs over, the one named last changes fastest.
Arguments:
- attn_partial: bfloat16 [4, 512, 7168], P('tp', 'dp'), may hold values from -3 to 3
- hidden_in: bfloat16 [512, 7168], P('dp', 'tp'), may hold values from -6 to 6
- norm_gain: float32 [7168], replicated, may hold values from 0.5 to 1.5
- expert_ids: int32 [512, 8], P('dp'), may hold values from 0 to 255, all different within a row; in each aligned block of 64 rows (0 to 63, 64 to 127, ...) at most 4 rows name the same one
- route_prob: bfloat16 [512, 8], P('dp'), may hold values from 0.049804688 to 0.3984375
- w_gate: bfloat16 [8, 7168, 1024], P('dp', None, 'tp'), may hold values from -0.0625 to 0.0625
- w_up: bfloat16 [8, 7168, 1024], P('dp', None, 'tp'), may hold values from -0.0625 to 0.0625
- w_down: bfloat16 [8, 1024, 7168], P('dp', 'tp'), may hold values from -0.1875 to 0.1875
Outputs:
- layer_out: bfloat16 [512, 7168], P('dp', 'tp')
- amax_input: float32 [8], P('dp')
- amax_hidden: float32 [8], P('dp')
The draws below stay inside these ranges and needn't reach their ends.
Inputs may be any that keep to these rules, and one draw needn't show every extreme that they name: `expert_ids`: each token names 8 different experts; within each aligned block of 64 tokens no expert is named by more than 4 tokens.
All inputs are finite; a program needn't handle non-finite values.
Results may differ from the reference program's by a relative error of at most 0.0075.
Values may be sent and summed in bfloat16 or wider, within the bound.
No kernel may reach another device: no remote copies, remote signals or barrier semaphores. Data moves between devices by JAX's collectives and lax.ppermute only.
A program may use at most 64 MiB of HBM per device.

```python
import math
import jax
import jax.numpy as jnp
import numpy as np
from jax import lax

MODEL_WIDTH = 7168
ROUTED = 256
TOP = 8
FF = 1024
TOK_DEV = 64
TOKENS = 512
GROUPS = 4
EXPERTS = 8
EXPERT_SLOTS = 4
N_DP = 8


def shard_levels(stream_key, shape, shards, smallest, high):
    level = 1.0
    for axis_at, shards_of in shards:
        heights = jax.random.uniform(jax.random.fold_in(jax.random.fold_in(stream_key, 6), axis_at), (shards_of,), jnp.float32, smallest / len(shards), high / len(shards))
        level = level * jnp.repeat(jnp.exp(heights), shape[axis_at] // shards_of).reshape((-1,) + (1,) * (len(shape) - 1 - axis_at))
    return level


def shared_out(own_key, own, number, rows, number_of, top, most, skew):
    sequence = jax.random.permutation(own_key, number_of)
    crowded, common = portions_of(number_of, rows * top, most, skew, True), portions_of(number_of, rows * top, most, skew, False)
    places = jnp.arange(number_of)

    def named(tallies, offset_by):
        used = int((tallies > 0).sum())
        fixed = max(1, used // 4)
        shifted = fixed + (places - fixed + offset_by * (used - fixed)) % max(1, number_of - fixed)
        return jnp.zeros((number_of,), jnp.int32).at[sequence[jnp.where(places < fixed, places, shifted)]].set(jnp.asarray(tallies, jnp.int32))

    tallies = jnp.where(number % 4 == 0, named(crowded, number // 4), named(common, number - number // 4 - 1))
    mixed = jax.random.permutation(jax.random.fold_in(own, 3), number_of)
    giver, sink = mixed[0:number_of // 2 * 2:2], mixed[1:number_of // 2 * 2:2]
    room = jnp.minimum(tallies[giver] - 1, most - tallies[sink]) // 2
    room = jnp.where((giver == sequence[0]) | (sink == sequence[0]) | (tallies[sink] == 0), 0, jnp.maximum(room, 0))
    shifted = jax.random.randint(jax.random.fold_in(own, 4), (number_of // 2,), 0, 1 << 20) % (room + 1)
    tallies = tallies.at[giver].add(-shifted).at[sink].add(shifted)
    items = jnp.searchsorted(jnp.cumsum(tallies), jnp.arange(rows * top), side="right").astype(jnp.int32)
    table = items.reshape(top, rows).T
    table = table[jax.random.permutation(jax.random.fold_in(own, 1), rows)]
    offset_by = jax.random.randint(jax.random.fold_in(own, 2), (rows, 1), 0, top)
    return jnp.take_along_axis(table, (jnp.arange(top)[None, :] + offset_by) % top, axis=1)


def portions_of(amount, total, bound, skew, full):
    portions = [(1 << 20) // math.isqrt(grade ** skew) + 1 for grade in range(1, amount + 1)]
    largest = bound if full else min(bound, max(-(-total // amount), total * portions[0] // sum(portions)))
    least = 1 if total - largest >= amount - 1 else 0
    counts, spare = [largest] + [least] * (amount - 1), total - largest - least * (amount - 1)
    while spare > 0:
        movable = [i for i in range(1, amount) if counts[i] < largest] or [i for i in range(1, amount) if counts[i] < bound]
        mass, budget = sum([portions[i] for i in movable]), spare
        for i in movable:
            extra = min(bound - counts[i], max(1, budget * portions[i] // mass), spare)
            counts[i] = counts[i] + extra
            spare = spare - extra
    return np.array(counts)


def gaussian(own_key, extent, spread, bound, cuts=(), kind=jnp.bfloat16):
    result = spread * jax.random.normal(own_key, extent, jnp.float32)
    if cuts:
        result = result * shard_levels(own_key, extent, cuts, -0.22, 0.18)
    return jnp.clip(result, -bound, bound).astype(kind)


def setup_inputs(seed: int = 0) -> dict:
    keys = jax.random.split(jax.random.key(seed), 9)
    attn_partial = gaussian(keys[0], (GROUPS, TOKENS, MODEL_WIDTH), 0.5, 3.0, ((0, 4), (1, 8)))
    hidden_in = gaussian(keys[1], (TOKENS, MODEL_WIDTH), 1.0, 6.0, ((0, 8), (1, 4)))
    norm_gain = jnp.clip(1.0 + 0.1 * jax.random.normal(keys[2], (MODEL_WIDTH,), jnp.float32), 0.5, 1.5)
    expert_ids_keys = jax.random.split(jax.random.fold_in(keys[3], 1), TOKENS // TOK_DEV)
    expert_ids_turns = jax.random.permutation(jax.random.fold_in(keys[3], 3), TOKENS // TOK_DEV)
    expert_ids = jax.vmap(lambda own, number: shared_out(jax.random.fold_in(keys[3], 2), own, number, TOK_DEV, ROUTED, TOP, EXPERT_SLOTS, 2))(expert_ids_keys, expert_ids_turns).reshape((TOKENS, TOP))
    route_prob = jnp.clip(0.049804688 + 0.3486328 * jax.random.uniform(keys[4], (TOKENS, TOP), jnp.float32) ** shard_levels(keys[4], (TOKENS, TOP), ((0, 8),), -0.2, 0.2), 0.049804688, 0.3984375).astype(jnp.bfloat16)
    w_gate = gaussian(keys[5], (EXPERTS, MODEL_WIDTH, FF), MODEL_WIDTH ** -0.5, 0.0625, ((0, 8), (2, 4)))
    w_up = gaussian(keys[6], (EXPERTS, MODEL_WIDTH, FF), MODEL_WIDTH ** -0.5, 0.0625, ((0, 8), (2, 4)))
    w_down = gaussian(keys[7], (EXPERTS, FF, MODEL_WIDTH), FF ** -0.5, 0.1875, ((0, 8), (1, 4)))
    return {"attn_partial": attn_partial, "hidden_in": hidden_in, "norm_gain": norm_gain, "expert_ids": expert_ids, "route_prob": route_prob, "w_gate": w_gate, "w_up": w_up, "w_down": w_down}


eps = 1e-06

def route_tables(ids_block, prob_block, experts, capacity):
    matches = ids_block[:, :, None] == jnp.arange(experts, dtype=jnp.int32)[None, None, :]
    onehot = lax.optimization_barrier(jnp.sum(matches.astype(jnp.int32), axis=1))
    weight = lax.optimization_barrier(jnp.sum(jnp.where(matches, prob_block[:, :, None].astype(jnp.float32), jnp.float32(0.0)), axis=1))
    before = jnp.cumsum(onehot, axis=0) - onehot
    placing = (onehot.T[:, None, :] == 1) & (before.T[:, None, :] == jnp.arange(capacity, dtype=jnp.int32)[None, :, None])
    return (placing, weight)

def reference(attn_partial, hidden_in, norm_gain, expert_ids, route_prob, w_gate, w_up, w_down):
    experts = N_DP
    residual = hidden_in.astype(jnp.float32) + lax.optimization_barrier(jnp.sum(attn_partial.astype(jnp.float32), axis=0))
    mean_sq = lax.optimization_barrier(jnp.mean(residual * residual, axis=1, keepdims=True))
    normed = (residual * lax.rsqrt(mean_sq + eps) * norm_gain).astype(jnp.bfloat16)
    ids_blocks = expert_ids.reshape(N_DP, TOK_DEV, TOP)
    probability_blocks = route_prob.reshape(N_DP, TOK_DEV, TOP)
    normalized_blocks = normed.reshape(N_DP, TOK_DEV, MODEL_WIDTH).astype(jnp.float32)
    placing, weight = jax.vmap(lambda ids_block, prob_block: route_tables(ids_block, prob_block, experts, EXPERT_SLOTS))(ids_blocks, probability_blocks)

    def expert(operands):
        selection_mask, gate_w, up_w, down_w = operands
        expert_slot_rows = jnp.einsum('jrn,jnf->jrf', selection_mask.astype(jnp.float32), normalized_blocks).astype(jnp.bfloat16).reshape(N_DP * EXPERT_SLOTS, MODEL_WIDTH)
        gate_val = jnp.dot(expert_slot_rows, gate_w, preferred_element_type=jnp.float32)
        up_val = jnp.dot(expert_slot_rows, up_w, preferred_element_type=jnp.float32)
        hidden_act = (jax.nn.silu(gate_val) * up_val).astype(jnp.bfloat16)
        expert_out = jnp.dot(hidden_act, down_w, preferred_element_type=jnp.float32)
        input_peak = jnp.max(jnp.abs(expert_slot_rows.astype(jnp.float32)))
        hidden_peak = jnp.max(jnp.abs(hidden_act.astype(jnp.float32)))
        return (expert_out.reshape(N_DP, EXPERT_SLOTS, MODEL_WIDTH), input_peak, hidden_peak)
    expert_outs, amax_input, amax_hidden = lax.map(expert, (jnp.swapaxes(placing, 0, 1), w_gate, w_up, w_down))

    def combine(operands):
        selection_mask, block_weight, returned = operands
        combine_matrix = (selection_mask.astype(jnp.float32) * block_weight.T[:, None, :]).reshape(experts * EXPERT_SLOTS, TOK_DEV)
        return jnp.dot(combine_matrix.T, returned.reshape(experts * EXPERT_SLOTS, MODEL_WIDTH), precision=lax.Precision.HIGHEST, preferred_element_type=jnp.float32)
    moe_out = lax.map(combine, (placing, weight, jnp.swapaxes(expert_outs, 0, 1)))
    layer_out = (residual + moe_out.reshape(TOKENS, MODEL_WIDTH)).astype(jnp.bfloat16)
    return (layer_out, amax_input, amax_hidden)
```

```python
import jax
import jax.numpy as jnp
from jax import lax
from jax.sharding import Mesh
from jax.sharding import PartitionSpec as P

EXPERT_SLOTS = 4
LANES = 128
eps = 1e-06
BF = jnp.bfloat16
F32 = jnp.float32


def route_tables(expert_ids, route_prob, experts, capacity):
    matches = expert_ids[:, :, None] == jnp.arange(experts, dtype=jnp.int32)[None, None, :]
    onehot = jnp.sum(matches.astype(jnp.int32), axis=1)
    weight = jnp.sum(jnp.where(matches, route_prob[:, :, None].astype(F32), F32(0.0)), axis=1)
    before = jnp.cumsum(onehot, axis=0) - onehot
    placing = (onehot.T[:, None, :] == 1) & (
        before.T[:, None, :] == jnp.arange(capacity, dtype=jnp.int32)[None, :, None]
    )
    return weight, placing


def shift(x, axis, by):
    n = lax.axis_size(axis)
    return lax.ppermute(x, axis, [(i, (i + by) % n) for i in range(n)])


def on_device(attn_partial, hidden_in, norm_gain, expert_ids, route_prob, w_gate, w_up, w_down):
    experts, his, los = lax.axis_size("dp"), lax.axis_size("hi"), lax.axis_size("lo")
    h, l = lax.axis_index("hi"), lax.axis_index("lo")
    tokens, cols = hidden_in.shape
    slots = experts * EXPERT_SLOTS
    partial = attn_partial[0]

    def piece(x, hh, ll):
        return lax.dynamic_slice_in_dim(x, (hh * los + ll) * cols, cols, 1)

    def half(x, ll):
        return jnp.concatenate([piece(x, hh, ll) for hh in range(his)], axis=1)

    pair = half(partial, l).astype(F32)
    for k in range(1, los):
        pair = pair + shift(half(partial, (l + k) % los), "lo", k).astype(F32)
    residual = lax.dynamic_slice_in_dim(pair, h * cols, cols, 1) + hidden_in.astype(F32)
    for k in range(1, his):
        out = lax.dynamic_slice_in_dim(pair, (h + k) % his * cols, cols, 1).astype(BF)
        residual = residual + shift(out, "hi", k).astype(F32)

    weight, placing = route_tables(expert_ids, route_prob, experts, EXPERT_SLOTS)
    selection = placing.reshape(slots, tokens).astype(BF)
    chosen = jnp.dot(selection, residual.astype(BF), preferred_element_type=F32).astype(BF)
    outgoing = jnp.broadcast_to(
        chosen.reshape(experts, 1, EXPERT_SLOTS, cols), (experts, his, EXPERT_SLOTS, cols)
    ).reshape(experts * his, EXPERT_SLOTS, cols)
    incoming = lax.all_to_all(outgoing, ("dp", "hi"), 0, 0, tiled=True)
    incoming = incoming.reshape(experts, his, EXPERT_SLOTS, cols)
    own = jnp.concatenate([incoming[:, hh].reshape(slots, cols) for hh in range(his)], axis=1)
    held = [own] + [shift(own, "lo", k) for k in range(1, los)]
    by_lo = []
    for ll in range(los):
        value = held[0]
        for k in range(1, los):
            value = jnp.where((l - ll) % los == k, held[k], value)
        by_lo.append(value)
    rows = jnp.concatenate(
        [by_lo[ll][:, hh * cols : (hh + 1) * cols] for hh in range(his) for ll in range(los)], axis=1
    ).astype(F32)
    mean_sq = jnp.mean(rows * rows, axis=1, keepdims=True)
    slot_rows = (rows * lax.rsqrt(mean_sq + eps) * norm_gain).astype(BF)
    gate_val = jnp.dot(slot_rows, w_gate[0], preferred_element_type=F32)
    up_val = jnp.dot(slot_rows, w_up[0], preferred_element_type=F32)
    hidden_act = (jax.nn.silu(gate_val) * up_val).astype(BF)
    partial_out = jnp.dot(hidden_act, w_down[0], preferred_element_type=F32)
    input_peak = jnp.max(jnp.abs(slot_rows.astype(F32)))
    hidden_peak = jnp.max(jnp.abs(hidden_act.astype(F32)))

    def tagged(x, peak):
        return jnp.concatenate([x.astype(BF), jnp.full((x.shape[0], LANES), peak, BF)], axis=1)

    total = half(partial_out, l)
    for k in range(1, los):
        got = shift(tagged(half(partial_out, (l + k) % los), hidden_peak), "lo", k)
        total = total + got[:, : his * cols].astype(F32)
        hidden_peak = jnp.maximum(hidden_peak, got[0, his * cols].astype(F32))
    back = jnp.stack(
        [
            tagged(total[:, hh * cols : (hh + 1) * cols], hidden_peak).reshape(
                experts, EXPERT_SLOTS, cols + LANES
            )
            for hh in range(his)
        ],
        axis=1,
    ).reshape(experts * his, EXPERT_SLOTS, cols + LANES)
    returned = lax.all_to_all(back, ("dp", "hi"), 0, 0, tiled=True)
    peaks = lax.dynamic_slice_in_dim(
        returned[:, 0, cols].reshape(experts, his), lax.axis_index("dp"), 1, 0
    )
    combine = (placing.astype(F32) * weight.T[:, None, :]).astype(BF)
    combine = jnp.broadcast_to(
        combine[:, None], (experts, his, EXPERT_SLOTS, tokens)
    ).reshape(slots * his, tokens)
    moe_out = jnp.dot(
        combine.T,
        returned[:, :, :cols].reshape(slots * his, cols),
        preferred_element_type=F32,
    )
    layer_out = (residual + moe_out).astype(BF)
    return layer_out, input_peak.reshape(1), jnp.max(peaks.astype(F32)).reshape(1)


def solution(mesh):
    tp = mesh.shape["tp"]
    lo = 2 if tp % 2 == 0 else 1
    split = Mesh(mesh.devices.reshape(mesh.shape["dp"], tp // lo, lo), ("dp", "hi", "lo"))
    tps = ("hi", "lo")
    placed = (
        P(tps, "dp", None),
        P("dp", tps),
        P(),
        P("dp", None),
        P("dp", None),
        P("dp", None, tps),
        P("dp", None, tps),
        P("dp", tps, None),
    )
    return jax.shard_map(
        on_device,
        mesh=split,
        in_specs=placed,
        out_specs=(P("dp", tps), P("dp"), P("dp")),
        check_vma=False,
    )
```

```python
import jax
import jax.numpy as jnp
from jax import lax
from jax.experimental import pallas as pl
from jax.experimental.pallas import tpu as pltpu
from jax.sharding import Mesh
from jax.sharding import PartitionSpec as P

EXPERT_SLOTS = 4
SUBLANES = 8
LANES = 128
SPLIT = SUBLANES // EXPERT_SLOTS
eps = 1e-06
BF = jnp.bfloat16
F32 = jnp.float32
HIGHEST = lax.Precision.HIGHEST
VMEM = pl.BlockSpec(memory_space=pltpu.VMEM)
SMEM = pl.BlockSpec(memory_space=pltpu.SMEM)
HBM = pl.BlockSpec(memory_space=pltpu.HBM)
MIB = 1 << 20


def dot(a, b, precision=None):
    return jnp.dot(a, b, precision=precision, preferred_element_type=F32)


def iota(shape, axis):
    return lax.broadcasted_iota(jnp.int32, shape, axis)


def shift(x, axis, by):
    n = lax.axis_size(axis)
    return lax.ppermute(x, axis, [(i, (i + by) % n) for i in range(n)])


def stay(*arrays):
    return [pltpu.with_memory_space_constraint(a, pltpu.HBM) for a in arrays]


def early_kernel(his, los, partial_ref, hidden_ref, ids_hbm, prob_hbm, *refs):
    own_ref, held_ref, pick_ref, comb_ref, ids_ref, prob_ref, small, large = refs
    cols = hidden_ref.shape[1]
    l = lax.axis_index("lo")
    first = [
        pltpu.make_async_copy(ids_hbm, ids_ref, small.at[0]),
        pltpu.make_async_copy(prob_hbm, prob_ref, small.at[1]),
    ]
    rest = [pltpu.make_async_copy(hidden_ref, held_ref, large.at[his])]
    for x in range(his):
        at = pl.multiple_of((x * los + l) * cols, LANES)
        rest.append(
            pltpu.make_async_copy(
                partial_ref.at[0, :, pl.ds(at, cols)], own_ref.at[x], large.at[x]
            )
        )
    for copy in first + rest:
        copy.start()
    for copy in first:
        copy.wait()
    names, tokens = ids_ref.shape
    rows, wide = pick_ref.shape[1], comb_ref.shape[2]
    experts = rows // SUBLANES
    ids, prob = ids_ref[...], prob_ref[...].astype(F32)
    expert = iota((experts, tokens), 0)
    match = jnp.zeros((experts, tokens), F32)
    weight = jnp.zeros((experts, tokens), F32)
    for k in range(names):
        same = ids[k : k + 1] == expert
        match = match + jnp.where(same, 1.0, 0.0)
        weight = weight + jnp.where(same, prob[k : k + 1], 0.0)
    earlier = jnp.where(iota((tokens, tokens), 0) < iota((tokens, tokens), 1), 1.0, 0.0)
    slot = jnp.where(match > 0.0, dot(match, earlier, HIGHEST), -1.0)

    def spread(x, count, per):
        owner = jnp.where(iota((count, experts), 0) // per == iota((count, experts), 1), 1.0, 0.0)
        return dot(owner, x, HIGHEST)

    at = iota((rows, tokens), 0)
    slots = spread(slot, rows, SUBLANES)
    for s in range(SPLIT):
        here = (slots == (at % EXPERT_SLOTS).astype(F32)) & (at // EXPERT_SLOTS % SPLIT == s)
        pick_ref[s] = jnp.where(here, 1.0, 0.0).astype(BF)
    at = iota((wide, tokens), 0)
    slots, weights = spread(slot, wide, his * SUBLANES), spread(weight, wide, his * SUBLANES)
    for s in range(SPLIT):
        here = (slots == (at % EXPERT_SLOTS).astype(F32)) & (at // EXPERT_SLOTS % SPLIT == s)
        comb_ref[s] = jnp.where(here, weights, 0.0).T.astype(BF)
    for copy in rest:
        copy.wait()


def choose_kernel(los, pick_ref, own_ref, *refs):
    others, sel_ref, res_ref = refs[: los - 1], refs[los - 1], refs[los]
    his, _, cols = own_ref.shape
    width = cols // SPLIT
    h, l = lax.axis_index("hi"), lax.axis_index("lo")
    for k in range(1, his):
        hh = lax.rem(h + k, his)
        pair = own_ref[hh].astype(F32)
        at = pl.multiple_of((hh * los + l) * cols, LANES)
        for other in others:
            pair = pair + other[:, pl.ds(at, cols)].astype(F32)
        pair = pair.astype(BF)
        res_ref[k - 1] = pair
        chosen = dot(pick_ref[0], pair[:, :width])
        for s in range(1, SPLIT):
            chosen = chosen + dot(pick_ref[s], pair[:, s * width : (s + 1) * width])
        sel_ref[k - 1] = chosen.astype(BF)


def load_kernel(los, *refs):
    gain_hbm, wg_hbm, wu_hbm, hidden_ref, pick_ref, own_ref = refs[:6]
    others = refs[6 : 5 + los]
    gain_ref, wg_ref, wu_ref, mine_ref, sel_ref, sems = refs[5 + los :]
    copies = [
        pltpu.make_async_copy(wg_hbm, wg_ref, sems.at[0]),
        pltpu.make_async_copy(wu_hbm, wu_ref, sems.at[1]),
        pltpu.make_async_copy(gain_hbm, gain_ref, sems.at[2]),
    ]
    for copy in copies:
        copy.start()
    _, cols = hidden_ref.shape
    width = cols // SPLIT
    h, l = lax.axis_index("hi"), lax.axis_index("lo")
    mine = hidden_ref[...].astype(F32) + own_ref[h].astype(F32)
    at = pl.multiple_of((h * los + l) * cols, LANES)
    for other in others:
        mine = mine + other[:, pl.ds(at, cols)].astype(F32)
    mine_ref[...] = mine
    chosen = dot(pick_ref[0].astype(F32), mine[:, :width], HIGHEST)
    for s in range(1, SPLIT):
        chosen = chosen + dot(
            pick_ref[s].astype(F32), mine[:, s * width : (s + 1) * width], HIGHEST
        )
    sel_ref[...] = chosen
    for copy in copies:
        copy.wait()


def dispatch_kernel(n, sel_ref, *refs):
    gots, out_ref = refs[:n], refs[n]
    experts, his, subs, width = out_ref.shape
    chosen = sel_ref[...]
    for got in gots:
        chosen = chosen + got[...].astype(F32)
    chosen = chosen.astype(BF).reshape(experts, subs, width)
    for x in range(his):
        out_ref[:, x] = chosen


def regroup(even, odd):
    top = iota(even.shape, 0) < EXPERT_SLOTS
    return (
        jnp.where(top, even, pltpu.roll(odd, EXPERT_SLOTS, 0)),
        jnp.where(top, pltpu.roll(even, EXPERT_SLOTS, 0), odd),
    )


def gather_rows(ref, x, experts):
    his = ref.shape[0] // experts
    low, high = [], []
    for p in range(0, experts, SPLIT):
        even, odd = ref[p * his + x].astype(F32), ref[(p + 1) * his + x].astype(F32)
        first, second = regroup(even, odd)
        low.append(first)
        high.append(second)
    return jnp.concatenate(
        [jnp.concatenate(low, axis=0), jnp.concatenate(high, axis=0)], axis=1
    )


def products(los, helds, gain_ref, wg_ref, wu_ref, gate, up, square, top):
    l, experts = lax.axis_index("lo"), lax.axis_size("dp")
    for k, held in helds:
        his = held.shape[0] // experts
        cols = SPLIT * held.shape[2]
        c = lax.rem(l - k + los, los)
        for x in range(his):
            value = gather_rows(held, x, experts)
            at = pl.multiple_of((x * los + c) * cols, LANES)
            square = square + jnp.sum(value * value, axis=1, keepdims=True)
            value = value * gain_ref[:, pl.ds(at, cols)]
            top = jnp.maximum(top, jnp.max(jnp.abs(value), axis=1, keepdims=True))
            value = value.astype(BF)
            gate = gate + dot(value, wg_ref[0, pl.ds(at, cols), :])
            up = up + dot(value, wu_ref[0, pl.ds(at, cols), :])
    return gate, up, square, top


def first_kernel(los, gain_ref, wg_ref, wu_ref, wd_hbm, held_ref, *refs):
    wd_ref, gate_ref, up_ref, square_ref, top_ref, sem = refs
    copy = pltpu.make_async_copy(wd_hbm, wd_ref, sem)
    copy.start()
    slots = gate_ref.shape[0]
    zero, none = jnp.zeros(gate_ref.shape, F32), jnp.zeros((slots, 1), F32)
    gate, up, square, top = products(
        los, [(0, held_ref)], gain_ref, wg_ref, wu_ref, zero, zero, none, none
    )
    gate_ref[...] = gate
    up_ref[...] = up
    square_ref[...] = jnp.broadcast_to(square, square_ref.shape)
    top_ref[...] = jnp.broadcast_to(top, top_ref.shape)
    copy.wait()


def down(act, wd_ref, his, los, c):
    cols = wd_ref.shape[2] // (his * los)
    for x in range(his):
        at = pl.multiple_of((x * los + c) * cols, LANES)
        yield slice(x * cols, (x + 1) * cols), dot(act, wd_ref[0, :, pl.ds(at, cols)])


def second_kernel(his, los, gain_ref, wg_ref, wu_ref, wd_ref, *refs):
    gate_ref, up_ref, square_ref, top_ref = refs[:4]
    helds = refs[4 : 3 + los]
    send_ref, act_ref, peak_ref, out_ref = refs[3 + los :]
    gate, up, square, top = products(
        los,
        list(enumerate(helds, 1)),
        gain_ref,
        wg_ref,
        wu_ref,
        gate_ref[...],
        up_ref[...],
        square_ref[:, :1],
        top_ref[:, :1],
    )
    scale = lax.rsqrt(square / wg_ref.shape[1] + eps)
    out_ref[0] = jnp.max(top * scale).astype(BF).astype(F32)
    gate, up = gate * scale, up * scale
    act = (gate / (1.0 + jnp.exp(-gate)) * up).astype(BF)
    act_ref[...] = act
    peak = jnp.max(jnp.abs(act.astype(F32)))
    peak_ref[...] = jnp.full(peak_ref.shape, peak, F32)
    l, slots = lax.axis_index("lo"), act.shape[0]
    for k in range(1, los):
        for cut, value in down(act, wd_ref, his, los, lax.rem(l + k, los)):
            send_ref[k - 1, :, cut] = value.astype(BF)
        send_ref[k - 1, :, -LANES:] = jnp.full((slots, LANES), peak, F32).astype(BF)


def third_kernel(his, los, act_ref, wd_ref, mine_ref, *refs):
    rests, keep_ref, res_ref = refs[: his - 1], refs[his - 1], refs[his]
    for cut, value in down(act_ref[...], wd_ref, his, los, lax.axis_index("lo")):
        keep_ref[:, cut] = value
    res = mine_ref[...]
    for rest in rests:
        res = res + rest[...].astype(F32)
    res_ref[...] = res


def pair_kernel(his, n, keep_ref, peak_ref, *refs):
    gots, out_ref = refs[:n], refs[n]
    blocks, subs, width = out_ref.shape
    width = width - LANES
    cols, experts = SPLIT * width, blocks // his
    peak = jnp.max(peak_ref[...])
    for got in gots:
        peak = jnp.maximum(peak, jnp.max(got[:, -LANES:].astype(F32)))
    for x in range(his):
        total = keep_ref[:, x * cols : (x + 1) * cols]
        for got in gots:
            total = total + got[:, x * cols : (x + 1) * cols].astype(F32)
        for p in range(0, experts, SPLIT):
            rows = slice(p * EXPERT_SLOTS, p * EXPERT_SLOTS + subs)
            even, odd = regroup(total[rows, :width], total[rows, width:])
            out_ref[p * his + x, :, :width] = even.astype(BF)
            out_ref[(p + 1) * his + x, :, :width] = odd.astype(BF)
    out_ref[:, :, width:] = jnp.full((blocks, subs, LANES), peak, F32).astype(BF)


def combine_kernel(res_ref, comb_ref, back_ref, out_ref, peak_ref):
    blocks, subs, width = back_ref.shape
    width = width - LANES
    experts = lax.axis_size("dp")
    his = blocks // experts
    back = back_ref[:, :, :width].reshape(blocks * subs, width)
    for s in range(SPLIT):
        cut = slice(s * width, (s + 1) * width)
        out_ref[:, cut] = (res_ref[:, cut] + dot(comb_ref[s], back)).astype(BF)
    peak = jnp.max(back_ref[pl.ds(lax.axis_index("dp") * his, his), :, width:].astype(F32))
    peak_ref[0] = peak


def call(kernel, mib, ins, outs, scratch=(), flops=0, moved=0):
    places = [SMEM if getattr(o, "memory_space", None) == pltpu.SMEM else VMEM for o in outs]
    return pl.pallas_call(
        kernel,
        out_shape=outs,
        in_specs=[HBM if at == "hbm" else VMEM for at, _ in ins],
        out_specs=places,
        scratch_shapes=scratch,
        compiler_params=pltpu.CompilerParams(vmem_limit_bytes=mib * MIB),
        cost_estimate=pl.CostEstimate(flops=flops, bytes_accessed=moved, transcendentals=0),
    )(*[stay(x)[0] if at == "hbm" else x for at, x in ins])


def near(*arrays):
    return [("vmem", a) for a in arrays]


def far(*arrays):
    return [("hbm", a) for a in arrays]


def on_device(attn_partial, hidden_in, norm_gain, expert_ids, route_prob, w_gate, w_up, w_down):
    experts, his, los = lax.axis_size("dp"), lax.axis_size("hi"), lax.axis_size("lo")
    tokens, cols = hidden_in.shape
    _, units = w_gate.shape[1:]
    width, blocks = cols // SPLIT, experts * his
    slots, rows = experts * EXPERT_SLOTS, experts * SUBLANES
    gain = norm_gain.reshape(1, -1)

    others = [shift(attn_partial[0], "lo", k) for k in range(1, los)]
    own, hidden, pick, comb = call(
        lambda *refs: early_kernel(his, los, *refs),
        4,
        far(attn_partial, hidden_in, expert_ids.T, route_prob.T),
        [
            pltpu.VMEM((his, tokens, cols), BF),
            pltpu.VMEM((tokens, cols), BF),
            pltpu.VMEM((SPLIT, rows, tokens), BF),
            pltpu.VMEM((SPLIT, tokens, blocks * SUBLANES), BF),
        ],
        [
            pltpu.VMEM(expert_ids.shape[::-1], expert_ids.dtype),
            pltpu.VMEM(route_prob.shape[::-1], route_prob.dtype),
            pltpu.SemaphoreType.DMA((2,)),
            pltpu.SemaphoreType.DMA((his + 1,)),
        ],
        moved=2 * MIB,
    )
    sels, rests = call(
        lambda *refs: choose_kernel(los, *refs),
        4,
        near(pick, own, *others),
        [
            pltpu.VMEM((his - 1, rows, width), BF),
            pltpu.VMEM((his - 1, tokens, cols), BF),
        ],
    )
    sels = [shift(sels[k - 1], "hi", k) for k in range(1, his)]
    rests = [shift(rests[k - 1], "hi", k) for k in range(1, his)]
    gain, wg, wu, mine, sel = call(
        lambda *refs: load_kernel(los, *refs),
        4,
        far(gain, w_gate, w_up) + near(hidden, pick, own, *others),
        [
            pltpu.VMEM(gain.shape, F32),
            pltpu.VMEM(w_gate.shape, BF),
            pltpu.VMEM(w_up.shape, BF),
            pltpu.VMEM((tokens, cols), F32),
            pltpu.VMEM((rows, width), F32),
        ],
        [pltpu.SemaphoreType.DMA((3,))],
        moved=8 * MIB,
    )
    (outgoing,) = call(
        lambda *refs: dispatch_kernel(his - 1, *refs),
        4,
        near(sel, *sels),
        [pltpu.VMEM((experts, his, SUBLANES, width), BF)],
    )
    incoming = lax.all_to_all(
        outgoing.reshape(blocks, SUBLANES, width), ("dp", "hi"), 0, 0, tiled=True
    )
    helds = [shift(incoming, "lo", k) for k in range(1, los)]
    wd, *sums = call(
        lambda *refs: first_kernel(los, *refs),
        12,
        near(gain, wg, wu) + far(w_down) + near(incoming),
        [
            pltpu.VMEM(w_down.shape, BF),
            pltpu.VMEM((slots, units), F32),
            pltpu.VMEM((slots, units), F32),
            pltpu.VMEM((slots, LANES), F32),
            pltpu.VMEM((slots, LANES), F32),
        ],
        [pltpu.SemaphoreType.DMA],
        moved=4 * MIB,
    )
    sends, act, peak, top = call(
        lambda *refs: second_kernel(his, los, *refs),
        12,
        near(gain, wg, wu, wd, *sums, *helds),
        [
            pltpu.VMEM((los - 1, slots, his * cols + LANES), BF),
            pltpu.VMEM((slots, units), BF),
            pltpu.VMEM((SUBLANES, LANES), F32),
            pltpu.SMEM((1,), F32),
        ],
    )
    sends = [shift(sends[k - 1], "lo", k) for k in range(1, los)]
    keep, residual = call(
        lambda *refs: third_kernel(his, los, *refs),
        8,
        near(act, wd, mine, *rests),
        [pltpu.VMEM((slots, his * cols), F32), pltpu.VMEM((tokens, cols), F32)],
        moved=2 * MIB,
    )
    (back,) = call(
        lambda *refs: pair_kernel(his, los - 1, *refs),
        4,
        near(keep, peak, *sends),
        [pltpu.VMEM((blocks, SUBLANES, width + LANES), BF)],
    )
    back = lax.all_to_all(back, ("dp", "hi"), 0, 0, tiled=True)
    layer_out, hidden_top = pl.pallas_call(
        combine_kernel,
        out_shape=[
            jax.ShapeDtypeStruct((tokens, cols), BF),
            jax.ShapeDtypeStruct((1,), F32),
        ],
        in_specs=[VMEM] * 3,
        out_specs=[VMEM, SMEM],
        compiler_params=pltpu.CompilerParams(vmem_limit_bytes=4 * MIB),
        name="combine",
    )(residual, comb, back)
    return layer_out, top, hidden_top


def solution(mesh):
    tp = mesh.shape["tp"]
    lo = 2 if tp % 2 == 0 else 1
    split = Mesh(mesh.devices.reshape(mesh.shape["dp"], tp // lo, lo), ("dp", "hi", "lo"))
    tps = ("hi", "lo")
    placed = (
        P(tps, "dp", None),
        P("dp", tps),
        P(),
        P("dp", None),
        P("dp", None),
        P("dp", None, tps),
        P("dp", None, tps),
        P("dp", tps, None),
    )

    return jax.shard_map(
        on_device,
        mesh=split,
        in_specs=placed,
        out_specs=(P("dp", tps), P("dp"), P("dp")),
        check_vma=False,
    )
```

```python
import jax
import jax.numpy as jnp
from jax import lax
from jax.experimental import pallas as pl
from jax.experimental.pallas import tpu as pltpu
from jax.sharding import Mesh
from jax.sharding import PartitionSpec as P

EXPERT_SLOTS = 4
SUBLANES = 8
LANES = 128
SPLIT = SUBLANES // EXPERT_SLOTS
eps = 1e-06
BF = jnp.bfloat16
F32 = jnp.float32
HIGHEST = lax.Precision.HIGHEST
VMEM = pl.BlockSpec(memory_space=pltpu.VMEM)
SMEM = pl.BlockSpec(memory_space=pltpu.SMEM)
HBM = pl.BlockSpec(memory_space=pltpu.HBM)
MIB = 1 << 20


def dot(a, b, precision=None):
    return jnp.dot(a, b, precision=precision, preferred_element_type=F32)


def iota(shape, axis):
    return lax.broadcasted_iota(jnp.int32, shape, axis)


def shift(x, axis, by):
    n = lax.axis_size(axis)
    return lax.ppermute(x, axis, [(i, (i + by) % n) for i in range(n)])


def stay(*arrays):
    return [pltpu.with_memory_space_constraint(a, pltpu.HBM) for a in arrays]


def early_kernel(his, los, partial_ref, hidden_ref, ids_hbm, prob_hbm, wd_hbm, *refs):
    own_ref, held_ref, pick_ref, comb_ref, wd_ref, ids_ref, prob_ref, small, large = refs
    cols = hidden_ref.shape[1]
    l = lax.axis_index("lo")
    first = [
        pltpu.make_async_copy(ids_hbm, ids_ref, small.at[0]),
        pltpu.make_async_copy(prob_hbm, prob_ref, small.at[1]),
    ]
    rest = [pltpu.make_async_copy(hidden_ref, held_ref, large.at[his])]
    for x in range(his):
        at = pl.multiple_of((x * los + l) * cols, LANES)
        rest.append(
            pltpu.make_async_copy(
                partial_ref.at[0, :, pl.ds(at, cols)], own_ref.at[x], large.at[x]
            )
        )
    rest.append(pltpu.make_async_copy(wd_hbm, wd_ref, large.at[his + 1]))
    for copy in first + rest:
        copy.start()
    for copy in first:
        copy.wait()
    names, tokens = ids_ref.shape
    rows, wide = pick_ref.shape[1], comb_ref.shape[2]
    experts = rows // SUBLANES
    ids, prob = ids_ref[...], prob_ref[...].astype(F32)
    expert = iota((experts, tokens), 0)
    match = jnp.zeros((experts, tokens), F32)
    weight = jnp.zeros((experts, tokens), F32)
    for k in range(names):
        same = ids[k : k + 1] == expert
        match = match + jnp.where(same, 1.0, 0.0)
        weight = weight + jnp.where(same, prob[k : k + 1], 0.0)
    earlier = jnp.where(iota((tokens, tokens), 0) < iota((tokens, tokens), 1), 1.0, 0.0)
    slot = jnp.where(match > 0.0, dot(match, earlier, HIGHEST), -1.0)

    def spread(x, count, per):
        owner = jnp.where(iota((count, experts), 0) // per == iota((count, experts), 1), 1.0, 0.0)
        return dot(owner, x, HIGHEST)

    at = iota((rows, tokens), 0)
    slots = spread(slot, rows, SUBLANES)
    for s in range(SPLIT):
        here = (slots == (at % EXPERT_SLOTS).astype(F32)) & (at // EXPERT_SLOTS % SPLIT == s)
        pick_ref[s] = jnp.where(here, 1.0, 0.0).astype(BF)
    at = iota((wide, tokens), 0)
    slots, weights = spread(slot, wide, his * SUBLANES), spread(weight, wide, his * SUBLANES)
    for s in range(SPLIT):
        here = (slots == (at % EXPERT_SLOTS).astype(F32)) & (at // EXPERT_SLOTS % SPLIT == s)
        comb_ref[s] = jnp.where(here, weights, 0.0).T.astype(BF)
    for copy in rest:
        copy.wait()


def choose_kernel(los, pick_ref, own_ref, *refs):
    others, sel_ref, res_ref = refs[: los - 1], refs[los - 1], refs[los]
    his, _, cols = own_ref.shape
    width = cols // SPLIT
    h, l = lax.axis_index("hi"), lax.axis_index("lo")
    for k in range(1, his):
        hh = lax.rem(h + k, his)
        pair = own_ref[hh].astype(F32)
        at = pl.multiple_of((hh * los + l) * cols, LANES)
        for other in others:
            pair = pair + other[:, pl.ds(at, cols)].astype(F32)
        pair = pair.astype(BF)
        res_ref[k - 1] = pair
        chosen = dot(pick_ref[0], pair[:, :width])
        for s in range(1, SPLIT):
            chosen = chosen + dot(pick_ref[s], pair[:, s * width : (s + 1) * width])
        sel_ref[k - 1] = chosen.astype(BF)


def load_kernel(los, *refs):
    gain_hbm, wg_hbm, wu_hbm, hidden_ref, pick_ref, own_ref = refs[:6]
    others = refs[6 : 5 + los]
    gain_ref, wg_ref, wu_ref, mine_ref, sel_ref, sems = refs[5 + los :]
    copies = [
        pltpu.make_async_copy(wg_hbm, wg_ref, sems.at[0]),
        pltpu.make_async_copy(wu_hbm, wu_ref, sems.at[1]),
        pltpu.make_async_copy(gain_hbm, gain_ref, sems.at[2]),
    ]
    for copy in copies:
        copy.start()
    _, cols = hidden_ref.shape
    width = cols // SPLIT
    h, l = lax.axis_index("hi"), lax.axis_index("lo")
    mine = hidden_ref[...].astype(F32) + own_ref[h].astype(F32)
    at = pl.multiple_of((h * los + l) * cols, LANES)
    for other in others:
        mine = mine + other[:, pl.ds(at, cols)].astype(F32)
    mine_ref[...] = mine
    chosen = dot(pick_ref[0].astype(F32), mine[:, :width], HIGHEST)
    for s in range(1, SPLIT):
        chosen = chosen + dot(
            pick_ref[s].astype(F32), mine[:, s * width : (s + 1) * width], HIGHEST
        )
    sel_ref[...] = chosen
    for copy in copies:
        copy.wait()


def dispatch_kernel(n, sel_ref, *refs):
    gots, out_ref = refs[:n], refs[n]
    experts, his, subs, width = out_ref.shape
    chosen = sel_ref[...]
    for got in gots:
        chosen = chosen + got[...].astype(F32)
    chosen = chosen.astype(BF).reshape(experts, subs, width)
    for x in range(his):
        out_ref[:, x] = chosen


def regroup(even, odd):
    top = iota(even.shape, 0) < EXPERT_SLOTS
    return (
        jnp.where(top, even, pltpu.roll(odd, EXPERT_SLOTS, 0)),
        jnp.where(top, pltpu.roll(even, EXPERT_SLOTS, 0), odd),
    )


def gather_rows(ref, x, experts):
    his = ref.shape[0] // experts
    low, high = [], []
    for p in range(0, experts, SPLIT):
        even, odd = ref[p * his + x].astype(F32), ref[(p + 1) * his + x].astype(F32)
        first, second = regroup(even, odd)
        low.append(first)
        high.append(second)
    return jnp.concatenate(
        [jnp.concatenate(low, axis=0), jnp.concatenate(high, axis=0)], axis=1
    )


def products(los, helds, gain_ref, wg_ref, wu_ref, gate, up, square, top):
    l, experts = lax.axis_index("lo"), lax.axis_size("dp")
    for k, held in helds:
        his = held.shape[0] // experts
        cols = SPLIT * held.shape[2]
        c = lax.rem(l - k + los, los)
        for x in range(his):
            value = gather_rows(held, x, experts)
            at = pl.multiple_of((x * los + c) * cols, LANES)
            square = square + jnp.sum(value * value, axis=1, keepdims=True)
            value = value * gain_ref[:, pl.ds(at, cols)]
            top = jnp.maximum(top, jnp.max(jnp.abs(value), axis=1, keepdims=True))
            value = value.astype(BF)
            gate = gate + dot(value, wg_ref[0, pl.ds(at, cols), :])
            up = up + dot(value, wu_ref[0, pl.ds(at, cols), :])
    return gate, up, square, top


def first_kernel(los, gain_ref, wg_ref, wu_ref, held_ref, *refs):
    gate_ref, up_ref, square_ref, top_ref = refs
    slots = gate_ref.shape[0]
    zero, none = jnp.zeros(gate_ref.shape, F32), jnp.zeros((slots, 1), F32)
    gate, up, square, top = products(
        los, [(0, held_ref)], gain_ref, wg_ref, wu_ref, zero, zero, none, none
    )
    gate_ref[...] = gate
    up_ref[...] = up
    square_ref[...] = jnp.broadcast_to(square, square_ref.shape)
    top_ref[...] = jnp.broadcast_to(top, top_ref.shape)


def down(act, wd_ref, his, los, c):
    cols = wd_ref.shape[2] // (his * los)
    for x in range(his):
        at = pl.multiple_of((x * los + c) * cols, LANES)
        yield slice(x * cols, (x + 1) * cols), dot(act, wd_ref[0, :, pl.ds(at, cols)])


def second_kernel(his, los, gain_ref, wg_ref, wu_ref, wd_ref, *refs):
    gate_ref, up_ref, square_ref, top_ref = refs[:4]
    helds = refs[4 : 3 + los]
    send_ref, act_ref, peak_ref, out_ref = refs[3 + los :]
    gate, up, square, top = products(
        los,
        list(enumerate(helds, 1)),
        gain_ref,
        wg_ref,
        wu_ref,
        gate_ref[...],
        up_ref[...],
        square_ref[:, :1],
        top_ref[:, :1],
    )
    scale = lax.rsqrt(square / wg_ref.shape[1] + eps)
    out_ref[0] = jnp.max(top * scale).astype(BF).astype(F32)
    gate, up = gate * scale, up * scale
    act = (gate / (1.0 + jnp.exp(-gate)) * up).astype(BF)
    act_ref[...] = act
    peak = jnp.max(jnp.abs(act.astype(F32)))
    peak_ref[...] = jnp.full(peak_ref.shape, peak, F32)
    l, slots = lax.axis_index("lo"), act.shape[0]
    for k in range(1, los):
        for cut, value in down(act, wd_ref, his, los, lax.rem(l + k, los)):
            send_ref[k - 1, :, cut] = value.astype(BF)
        send_ref[k - 1, :, -LANES:] = jnp.full((slots, LANES), peak, F32).astype(BF)


def third_kernel(his, los, act_ref, wd_ref, keep_ref):
    for cut, value in down(act_ref[...], wd_ref, his, los, lax.axis_index("lo")):
        keep_ref[:, cut] = value


def pair_kernel(his, n, keep_ref, peak_ref, *refs):
    gots, out_ref = refs[:n], refs[n]
    blocks, subs, width = out_ref.shape
    width = width - LANES
    cols, experts = SPLIT * width, blocks // his
    peak = jnp.max(peak_ref[...])
    for got in gots:
        peak = jnp.maximum(peak, jnp.max(got[:, -LANES:].astype(F32)))
    for x in range(his):
        total = keep_ref[:, x * cols : (x + 1) * cols]
        for got in gots:
            total = total + got[:, x * cols : (x + 1) * cols].astype(F32)
        for p in range(0, experts, SPLIT):
            rows = slice(p * EXPERT_SLOTS, p * EXPERT_SLOTS + subs)
            even, odd = regroup(total[rows, :width], total[rows, width:])
            out_ref[p * his + x, :, :width] = even.astype(BF)
            out_ref[(p + 1) * his + x, :, :width] = odd.astype(BF)
    out_ref[:, :, width:] = jnp.full((blocks, subs, LANES), peak, F32).astype(BF)


def peak_kernel(his, back_ref, peak_ref):
    peak = back_ref[pl.ds(lax.axis_index("dp") * his, his), :, -LANES:]
    peak_ref[0] = jnp.max(peak.astype(F32))


def combine_kernel(mine_ref, comb_ref, back_ref, *refs):
    rests, out_ref = refs[:-1], refs[-1]
    blocks, subs, width = back_ref.shape
    width = width - LANES
    back = back_ref[:, :, :width].reshape(blocks * subs, width)
    for s in range(SPLIT):
        cut = slice(s * width, (s + 1) * width)
        res = mine_ref[:, cut]
        for rest in rests:
            res = res + rest[:, cut].astype(F32)
        out_ref[:, cut] = (res + dot(comb_ref[s], back)).astype(BF)


def call(kernel, mib, ins, outs, scratch=(), flops=0, moved=0):
    places = [SMEM if isinstance(o, jax.ShapeDtypeStruct) else VMEM for o in outs]
    return pl.pallas_call(
        kernel,
        out_shape=outs,
        in_specs=[HBM if at == "hbm" else VMEM for at, _ in ins],
        out_specs=places,
        scratch_shapes=scratch,
        compiler_params=pltpu.CompilerParams(vmem_limit_bytes=mib * MIB),
        cost_estimate=pl.CostEstimate(flops=flops, bytes_accessed=moved, transcendentals=0),
    )(*[stay(x)[0] if at == "hbm" else x for at, x in ins])


def near(*arrays):
    return [("vmem", a) for a in arrays]


def far(*arrays):
    return [("hbm", a) for a in arrays]


def on_device(attn_partial, hidden_in, norm_gain, expert_ids, route_prob, w_gate, w_up, w_down):
    experts, his, los = lax.axis_size("dp"), lax.axis_size("hi"), lax.axis_size("lo")
    tokens, cols = hidden_in.shape
    _, units = w_gate.shape[1:]
    width, blocks = cols // SPLIT, experts * his
    slots, rows = experts * EXPERT_SLOTS, experts * SUBLANES
    gain = norm_gain.reshape(1, -1)

    others = [shift(attn_partial[0], "lo", k) for k in range(1, los)]
    own, hidden, pick, comb, wd = call(
        lambda *refs: early_kernel(his, los, *refs),
        4,
        far(attn_partial, hidden_in, expert_ids.T, route_prob.T, w_down),
        [
            pltpu.VMEM((his, tokens, cols), BF),
            pltpu.VMEM((tokens, cols), BF),
            pltpu.VMEM((SPLIT, rows, tokens), BF),
            pltpu.VMEM((SPLIT, tokens, blocks * SUBLANES), BF),
            pltpu.VMEM(w_down.shape, BF),
        ],
        [
            pltpu.VMEM(expert_ids.shape[::-1], expert_ids.dtype),
            pltpu.VMEM(route_prob.shape[::-1], route_prob.dtype),
            pltpu.SemaphoreType.DMA((2,)),
            pltpu.SemaphoreType.DMA((his + 2,)),
        ],
        moved=6 * MIB,
    )
    sels, rests = call(
        lambda *refs: choose_kernel(los, *refs),
        4,
        near(pick, own, *others),
        [
            pltpu.VMEM((his - 1, rows, width), BF),
            pltpu.VMEM((his - 1, tokens, cols), BF),
        ],
    )
    sels = [shift(sels[k - 1], "hi", k) for k in range(1, his)]
    gain, wg, wu, mine, sel = call(
        lambda *refs: load_kernel(los, *refs),
        4,
        far(gain, w_gate, w_up) + near(hidden, pick, own, *others),
        [
            pltpu.VMEM(gain.shape, F32),
            pltpu.VMEM(w_gate.shape, BF),
            pltpu.VMEM(w_up.shape, BF),
            pltpu.VMEM((tokens, cols), F32),
            pltpu.VMEM((rows, width), F32),
        ],
        [pltpu.SemaphoreType.DMA((3,))],
        moved=8 * MIB,
    )
    (outgoing,) = call(
        lambda *refs: dispatch_kernel(his - 1, *refs),
        4,
        near(sel, *sels),
        [pltpu.VMEM((experts, his, SUBLANES, width), BF)],
    )
    incoming = lax.all_to_all(
        outgoing.reshape(blocks, SUBLANES, width), ("dp", "hi"), 0, 0, tiled=True
    )
    helds = [shift(incoming, "lo", k) for k in range(1, los)]
    sums = call(
        lambda *refs: first_kernel(los, *refs),
        8,
        near(gain, wg, wu, incoming),
        [
            pltpu.VMEM((slots, units), F32),
            pltpu.VMEM((slots, units), F32),
            pltpu.VMEM((slots, LANES), F32),
            pltpu.VMEM((slots, LANES), F32),
        ],
        moved=4 * MIB,
    )
    sends, act, peak, top = call(
        lambda *refs: second_kernel(his, los, *refs),
        12,
        near(gain, wg, wu, wd, *sums, *helds),
        [
            pltpu.VMEM((los - 1, slots, his * cols + LANES), BF),
            pltpu.VMEM((slots, units), BF),
            pltpu.VMEM((SUBLANES, LANES), F32),
            jax.ShapeDtypeStruct((1,), F32),
        ],
    )
    sends = [shift(sends[k - 1], "lo", k) for k in range(1, los)]
    rests = [shift(rests[k - 1], "hi", k) for k in range(1, his)]
    (keep,) = call(
        lambda *refs: third_kernel(his, los, *refs),
        8,
        near(act, wd),
        [pltpu.VMEM((slots, his * cols), F32)],
        moved=2 * MIB,
    )
    (back,) = call(
        lambda *refs: pair_kernel(his, los - 1, *refs),
        4,
        near(keep, peak, *sends),
        [pltpu.VMEM((blocks, SUBLANES, width + LANES), BF)],
    )
    back = lax.all_to_all(back, ("dp", "hi"), 0, 0, tiled=True)
    (hidden_top,) = call(
        lambda *refs: peak_kernel(his, *refs),
        1,
        near(back),
        [jax.ShapeDtypeStruct((1,), F32)],
    )
    layer_out = pl.pallas_call(
        combine_kernel,
        out_shape=jax.ShapeDtypeStruct((tokens, cols), BF),
        in_specs=[VMEM] * (2 + his),
        out_specs=VMEM,
        compiler_params=pltpu.CompilerParams(vmem_limit_bytes=4 * MIB),
        name="combine",
    )(mine, comb, back, *rests)
    return layer_out, top, hidden_top


def solution(mesh):
    tp = mesh.shape["tp"]
    lo = 2 if tp % 2 == 0 else 1
    split = Mesh(mesh.devices.reshape(mesh.shape["dp"], tp // lo, lo), ("dp", "hi", "lo"))
    tps = ("hi", "lo")
    placed = (
        P(tps, "dp", None),
        P("dp", tps),
        P(),
        P("dp", None),
        P("dp", None),
        P("dp", None, tps),
        P("dp", None, tps),
        P("dp", tps, None),
    )

    return jax.shard_map(
        on_device,
        mesh=split,
        in_specs=placed,
        out_specs=(P("dp", tps), P("dp"), P("dp")),
        check_vma=False,
    )
```

```python
import jax
import jax.numpy as jnp
from jax import lax
from jax.experimental import pallas as pl
from jax.experimental.pallas import tpu as pltpu
from jax.sharding import Mesh
from jax.sharding import PartitionSpec as P

EXPERT_SLOTS = 4
SUBLANES = 8
LANES = 128
SPLIT = SUBLANES // EXPERT_SLOTS
eps = 1e-06
BF = jnp.bfloat16
F32 = jnp.float32
HIGHEST = lax.Precision.HIGHEST
VMEM = pl.BlockSpec(memory_space=pltpu.VMEM)
SMEM = pl.BlockSpec(memory_space=pltpu.SMEM)
HBM = pl.BlockSpec(memory_space=pltpu.HBM)
MIB = 1 << 20


def dot(a, b, precision=None):
    return jnp.dot(a, b, precision=precision, preferred_element_type=F32)


def iota(shape, axis):
    return lax.broadcasted_iota(jnp.int32, shape, axis)


def shift(x, axis, by):
    n = lax.axis_size(axis)
    return lax.ppermute(x, axis, [(i, (i + by) % n) for i in range(n)])


def stay(*arrays):
    return [pltpu.with_memory_space_constraint(a, pltpu.HBM) for a in arrays]


def cut_kernel(his, los, partial_ref, out_ref, sems):
    cols = out_ref.shape[3]
    l = lax.axis_index("lo")
    copies = []
    for k in range(1, los):
        for x in range(his):
            at = pl.multiple_of((x * los + lax.rem(l + k, los)) * cols, LANES)
            copies.append(
                pltpu.make_async_copy(
                    partial_ref.at[0, :, pl.ds(at, cols)], out_ref.at[k - 1, x], sems.at[k - 1, x]
                )
            )
    for copy in copies:
        copy.start()
    for copy in copies:
        copy.wait()


def early_kernel(his, los, partial_ref, hidden_ref, ids_hbm, prob_hbm, *refs):
    own_ref, held_ref, pick_ref, comb_ref, ids_ref, prob_ref, small, large = refs
    cols = hidden_ref.shape[1]
    l = lax.axis_index("lo")
    first = [
        pltpu.make_async_copy(ids_hbm, ids_ref, small.at[0]),
        pltpu.make_async_copy(prob_hbm, prob_ref, small.at[1]),
    ]
    rest = [pltpu.make_async_copy(hidden_ref, held_ref, large.at[his])]
    for x in range(his):
        at = pl.multiple_of((x * los + l) * cols, LANES)
        rest.append(
            pltpu.make_async_copy(
                partial_ref.at[0, :, pl.ds(at, cols)], own_ref.at[x], large.at[x]
            )
        )
    for copy in first + rest:
        copy.start()
    for copy in first:
        copy.wait()
    names, tokens = ids_ref.shape
    rows, wide = pick_ref.shape[1], comb_ref.shape[2]
    experts = rows // SUBLANES
    ids, prob = ids_ref[...], prob_ref[...].astype(F32)
    expert = iota((experts, tokens), 0)
    match = jnp.zeros((experts, tokens), F32)
    weight = jnp.zeros((experts, tokens), F32)
    for k in range(names):
        same = ids[k : k + 1] == expert
        match = match + jnp.where(same, 1.0, 0.0)
        weight = weight + jnp.where(same, prob[k : k + 1], 0.0)
    earlier = jnp.where(iota((tokens, tokens), 0) < iota((tokens, tokens), 1), 1.0, 0.0)
    slot = jnp.where(match > 0.0, dot(match, earlier, HIGHEST), -1.0)

    def spread(x, count, per):
        owner = jnp.where(iota((count, experts), 0) // per == iota((count, experts), 1), 1.0, 0.0)
        return dot(owner, x, HIGHEST)

    at = iota((rows, tokens), 0)
    slots = spread(slot, rows, SUBLANES)
    for s in range(SPLIT):
        here = (slots == (at % EXPERT_SLOTS).astype(F32)) & (at // EXPERT_SLOTS % SPLIT == s)
        pick_ref[s] = jnp.where(here, 1.0, 0.0).astype(BF)
    at = iota((wide, tokens), 0)
    slots, weights = spread(slot, wide, his * SUBLANES), spread(weight, wide, his * SUBLANES)
    for s in range(SPLIT):
        here = (slots == (at % EXPERT_SLOTS).astype(F32)) & (at // EXPERT_SLOTS % SPLIT == s)
        comb_ref[s] = jnp.where(here, weights, 0.0).T.astype(BF)
    for copy in rest:
        copy.wait()


def choose_kernel(los, pick_ref, own_ref, *refs):
    others, sel_ref, res_ref = refs[: los - 1], refs[los - 1], refs[los]
    his, _, cols = own_ref.shape
    width = cols // SPLIT
    h = lax.axis_index("hi")
    for k in range(1, his):
        hh = lax.rem(h + k, his)
        pair = own_ref[hh].astype(F32)
        for other in others:
            pair = pair + other[hh].astype(F32)
        pair = pair.astype(BF)
        res_ref[k - 1] = pair
        chosen = dot(pick_ref[0], pair[:, :width])
        for s in range(1, SPLIT):
            chosen = chosen + dot(pick_ref[s], pair[:, s * width : (s + 1) * width])
        sel_ref[k - 1] = chosen.astype(BF)


def load_kernel(los, *refs):
    hbms, (hidden_ref, pick_ref, own_ref) = refs[:4], refs[4:7]
    others, (mine_ref, sel_ref), sems = refs[7 : 6 + los], refs[10 + los : 12 + los], refs[-1]
    copies = [
        pltpu.make_async_copy(hbm, vmem, sems.at[i])
        for i, (hbm, vmem) in enumerate(zip(hbms, refs[6 + los : 10 + los]))
    ]
    for copy in copies:
        copy.start()
    cols = hidden_ref.shape[1]
    width = cols // SPLIT
    h = lax.axis_index("hi")
    mine = hidden_ref[...].astype(F32) + own_ref[h].astype(F32)
    for other in others:
        mine = mine + other[h].astype(F32)
    mine_ref[...] = mine
    chosen = dot(pick_ref[0].astype(F32), mine[:, :width], HIGHEST)
    for s in range(1, SPLIT):
        chosen = chosen + dot(
            pick_ref[s].astype(F32), mine[:, s * width : (s + 1) * width], HIGHEST
        )
    sel_ref[...] = chosen
    for copy in copies:
        copy.wait()


def dispatch_kernel(n, sel_ref, *refs):
    gots, out_ref = refs[:n], refs[n]
    experts, his, subs, width = out_ref.shape
    chosen = sel_ref[...]
    for got in gots:
        chosen = chosen + got[...].astype(F32)
    chosen = chosen.astype(BF).reshape(experts, subs, width)
    for x in range(his):
        out_ref[:, x] = chosen


def regroup(even, odd):
    top = iota(even.shape, 0) < EXPERT_SLOTS
    return (
        jnp.where(top, even, pltpu.roll(odd, EXPERT_SLOTS, 0)),
        jnp.where(top, pltpu.roll(even, EXPERT_SLOTS, 0), odd),
    )


def gather_rows(ref, x, experts):
    his = ref.shape[0] // experts
    low, high = [], []
    for p in range(0, experts, SPLIT):
        even, odd = ref[p * his + x].astype(F32), ref[(p + 1) * his + x].astype(F32)
        first, second = regroup(even, odd)
        low.append(first)
        high.append(second)
    return jnp.concatenate(
        [jnp.concatenate(low, axis=0), jnp.concatenate(high, axis=0)], axis=1
    )


def products(los, helds, gain_ref, wg_ref, wu_ref, gate, up, square, top):
    l, experts = lax.axis_index("lo"), lax.axis_size("dp")
    for k, held in helds:
        his = held.shape[0] // experts
        cols = SPLIT * held.shape[2]
        c = lax.rem(l - k + los, los)
        for x in range(his):
            value = gather_rows(held, x, experts)
            at = pl.multiple_of((x * los + c) * cols, LANES)
            square = square + jnp.sum(value * value, axis=1, keepdims=True)
            value = value * gain_ref[:, pl.ds(at, cols)]
            top = jnp.maximum(top, jnp.max(jnp.abs(value), axis=1, keepdims=True))
            value = value.astype(BF)
            gate = gate + dot(value, wg_ref[0, pl.ds(at, cols), :])
            up = up + dot(value, wu_ref[0, pl.ds(at, cols), :])
    return gate, up, square, top


def first_kernel(los, gain_ref, wg_ref, wu_ref, held_ref, *refs):
    gate_ref, up_ref, square_ref, top_ref = refs
    slots = gate_ref.shape[0]
    zero, none = jnp.zeros(gate_ref.shape, F32), jnp.zeros((slots, 1), F32)
    gate, up, square, top = products(
        los, [(0, held_ref)], gain_ref, wg_ref, wu_ref, zero, zero, none, none
    )
    gate_ref[...] = gate
    up_ref[...] = up
    square_ref[...] = jnp.broadcast_to(square, square_ref.shape)
    top_ref[...] = jnp.broadcast_to(top, top_ref.shape)


def down(act, wd_ref, his, los, c):
    cols = wd_ref.shape[2] // (his * los)
    for x in range(his):
        at = pl.multiple_of((x * los + c) * cols, LANES)
        yield slice(x * cols, (x + 1) * cols), dot(act, wd_ref[0, :, pl.ds(at, cols)])


def second_kernel(his, los, gain_ref, wg_ref, wu_ref, wd_ref, *refs):
    gate_ref, up_ref, square_ref, top_ref = refs[:4]
    helds = refs[4 : 3 + los]
    send_ref, act_ref, peak_ref, out_ref = refs[3 + los :]
    gate, up, square, top = products(
        los,
        list(enumerate(helds, 1)),
        gain_ref,
        wg_ref,
        wu_ref,
        gate_ref[...],
        up_ref[...],
        square_ref[:, :1],
        top_ref[:, :1],
    )
    scale = lax.rsqrt(square / wg_ref.shape[1] + eps)
    out_ref[0] = jnp.max(top * scale).astype(BF).astype(F32)
    gate, up = gate * scale, up * scale
    act = (gate / (1.0 + jnp.exp(-gate)) * up).astype(BF)
    act_ref[...] = act
    peak = jnp.max(jnp.abs(act.astype(F32)))
    peak_ref[...] = jnp.full(peak_ref.shape, peak, F32)
    l, slots = lax.axis_index("lo"), act.shape[0]
    for k in range(1, los):
        for cut, value in down(act, wd_ref, his, los, lax.rem(l + k, los)):
            send_ref[k - 1, :, cut] = value.astype(BF)
        send_ref[k - 1, :, -LANES:] = jnp.full((slots, LANES), peak, F32).astype(BF)


def third_kernel(his, los, act_ref, wd_ref, keep_ref):
    for cut, value in down(act_ref[...], wd_ref, his, los, lax.axis_index("lo")):
        keep_ref[:, cut] = value


def pair_kernel(his, n, keep_ref, peak_ref, *refs):
    gots, out_ref = refs[:n], refs[n]
    blocks, subs, width = out_ref.shape
    width = width - LANES
    cols, experts = SPLIT * width, blocks // his
    peak = jnp.max(peak_ref[...])
    for got in gots:
        peak = jnp.maximum(peak, jnp.max(got[:, -LANES:].astype(F32)))
    for x in range(his):
        total = keep_ref[:, x * cols : (x + 1) * cols]
        for got in gots:
            total = total + got[:, x * cols : (x + 1) * cols].astype(F32)
        for p in range(0, experts, SPLIT):
            rows = slice(p * EXPERT_SLOTS, p * EXPERT_SLOTS + subs)
            even, odd = regroup(total[rows, :width], total[rows, width:])
            out_ref[p * his + x, :, :width] = even.astype(BF)
            out_ref[(p + 1) * his + x, :, :width] = odd.astype(BF)
    out_ref[:, :, width:] = jnp.full((blocks, subs, LANES), peak, F32).astype(BF)


def peak_kernel(his, back_ref, peak_ref):
    peak = back_ref[pl.ds(lax.axis_index("dp") * his, his), :, -LANES:].astype(F32)
    peak_ref[...] = jnp.max(peak, axis=0)


def combine_kernel(mine_ref, comb_ref, back_ref, tile_ref, *refs):
    rests, (out_hbm, peak_ref, out_ref, sems) = refs[:-4], refs[-4:]
    blocks, subs, width = back_ref.shape
    width = width - LANES
    back = back_ref[:, :, :width].reshape(blocks * subs, width)
    copies = []
    for s in range(SPLIT):
        cut = slice(s * width, (s + 1) * width)
        res = mine_ref[:, cut]
        for rest in rests:
            res = res + rest[:, cut].astype(F32)
        out_ref[:, cut] = (res + dot(comb_ref[s], back)).astype(BF)
        copies.append(pltpu.make_async_copy(out_ref.at[:, cut], out_hbm.at[:, cut], sems.at[s]))
        copies[-1].start()
    peak_ref[0] = jnp.max(tile_ref[...])
    for copy in copies:
        copy.wait()


def call(kernel, mib, ins, outs, scratch=(), flops=0, moved=0):
    places = [SMEM if isinstance(o, jax.ShapeDtypeStruct) else VMEM for o in outs]
    return pl.pallas_call(
        kernel,
        out_shape=outs,
        in_specs=[HBM if at == "hbm" else VMEM for at, _ in ins],
        out_specs=places,
        scratch_shapes=scratch,
        compiler_params=pltpu.CompilerParams(vmem_limit_bytes=mib * MIB),
        cost_estimate=pl.CostEstimate(flops=flops, bytes_accessed=moved, transcendentals=0),
    )(*[stay(x)[0] if at == "hbm" else x for at, x in ins])


def near(*arrays):
    return [("vmem", a) for a in arrays]


def far(*arrays):
    return [("hbm", a) for a in arrays]


def on_device(attn_partial, hidden_in, norm_gain, expert_ids, route_prob, w_gate, w_up, w_down):
    experts, his, los = lax.axis_size("dp"), lax.axis_size("hi"), lax.axis_size("lo")
    tokens, cols = hidden_in.shape
    _, units = w_gate.shape[1:]
    width, blocks = cols // SPLIT, experts * his
    slots, rows = experts * EXPERT_SLOTS, experts * SUBLANES
    gain = norm_gain.reshape(1, -1)

    (cut,) = call(
        lambda *refs: cut_kernel(his, los, *refs),
        1,
        far(attn_partial),
        [pltpu.VMEM((los - 1, his, tokens, cols), BF)],
        [pltpu.SemaphoreType.DMA((los - 1, his))],
    )
    others = [shift(cut[k - 1], "lo", k) for k in range(1, los)]
    own, hidden, pick, comb = call(
        lambda *refs: early_kernel(his, los, *refs),
        4,
        far(attn_partial, hidden_in, expert_ids.T, route_prob.T),
        [
            pltpu.VMEM((his, tokens, cols), BF),
            pltpu.VMEM((tokens, cols), BF),
            pltpu.VMEM((SPLIT, rows, tokens), BF),
            pltpu.VMEM((SPLIT, tokens, blocks * SUBLANES), BF),
        ],
        [
            pltpu.VMEM(expert_ids.shape[::-1], expert_ids.dtype),
            pltpu.VMEM(route_prob.shape[::-1], route_prob.dtype),
            pltpu.SemaphoreType.DMA((2,)),
            pltpu.SemaphoreType.DMA((his + 1,)),
        ],
        moved=MIB,
    )
    sels, rests = call(
        lambda *refs: choose_kernel(los, *refs),
        4,
        near(pick, own, *others),
        [
            pltpu.VMEM((his - 1, rows, width), BF),
            pltpu.VMEM((his - 1, tokens, cols), BF),
        ],
    )
    sels = [shift(sels[k - 1], "hi", k) for k in range(1, his)]
    gain, wg, wu, wd, mine, sel = call(
        lambda *refs: load_kernel(los, *refs),
        4,
        far(gain, w_gate, w_up, w_down) + near(hidden, pick, own, *others),
        [
            pltpu.VMEM(gain.shape, F32),
            pltpu.VMEM(w_gate.shape, BF),
            pltpu.VMEM(w_up.shape, BF),
            pltpu.VMEM(w_down.shape, BF),
            pltpu.VMEM((tokens, cols), F32),
            pltpu.VMEM((rows, width), F32),
        ],
        [pltpu.SemaphoreType.DMA((4,))],
        moved=12 * MIB,
    )
    rests = [shift(rests[k - 1], "hi", k) for k in range(1, his)]
    (outgoing,) = call(
        lambda *refs: dispatch_kernel(his - 1, *refs),
        4,
        near(sel, *sels),
        [pltpu.VMEM((experts, his, SUBLANES, width), BF)],
    )
    incoming = lax.all_to_all(
        outgoing.reshape(blocks, SUBLANES, width), ("dp", "hi"), 0, 0, tiled=True
    )
    helds = [shift(incoming, "lo", k) for k in range(1, los)]
    sums = call(
        lambda *refs: first_kernel(los, *refs),
        8,
        near(gain, wg, wu, incoming),
        [
            pltpu.VMEM((slots, units), F32),
            pltpu.VMEM((slots, units), F32),
            pltpu.VMEM((slots, LANES), F32),
            pltpu.VMEM((slots, LANES), F32),
        ],
        moved=4 * MIB,
    )
    sends, act, peak, top = call(
        lambda *refs: second_kernel(his, los, *refs),
        12,
        near(gain, wg, wu, wd, *sums, *helds),
        [
            pltpu.VMEM((los - 1, slots, his * cols + LANES), BF),
            pltpu.VMEM((slots, units), BF),
            pltpu.VMEM((SUBLANES, LANES), F32),
            jax.ShapeDtypeStruct((1,), F32),
        ],
    )
    sends = [shift(sends[k - 1], "lo", k) for k in range(1, los)]
    (keep,) = call(
        lambda *refs: third_kernel(his, los, *refs),
        8,
        near(act, wd),
        [pltpu.VMEM((slots, his * cols), F32)],
        moved=2 * MIB,
    )
    (back,) = call(
        lambda *refs: pair_kernel(his, los - 1, *refs),
        4,
        near(keep, peak, *sends),
        [pltpu.VMEM((blocks, SUBLANES, width + LANES), BF)],
    )
    back = lax.all_to_all(back, ("dp", "hi"), 0, 0, tiled=True)
    (tile,) = call(
        lambda *refs: peak_kernel(his, *refs), 1, near(back), [pltpu.VMEM((SUBLANES, LANES), F32)]
    )
    layer_out, hidden_top = pl.pallas_call(
        combine_kernel,
        out_shape=[
            jax.ShapeDtypeStruct((tokens, cols), BF),
            jax.ShapeDtypeStruct((1,), F32),
        ],
        in_specs=[VMEM] * (3 + his),
        out_specs=[HBM, SMEM],
        scratch_shapes=[pltpu.VMEM((tokens, cols), BF), pltpu.SemaphoreType.DMA((SPLIT,))],
        compiler_params=pltpu.CompilerParams(vmem_limit_bytes=4 * MIB),
        name="combine",
    )(mine, comb, back, tile, *rests)
    return layer_out, top, hidden_top


def solution(mesh):
    tp = mesh.shape["tp"]
    lo = 2 if tp % 2 == 0 else 1
    split = Mesh(mesh.devices.reshape(mesh.shape["dp"], tp // lo, lo), ("dp", "hi", "lo"))
    tps = ("hi", "lo")
    placed = (
        P(tps, "dp", None),
        P("dp", tps),
        P(),
        P("dp", None),
        P("dp", None),
        P("dp", None, tps),
        P("dp", None, tps),
        P("dp", tps, None),
    )

    return jax.shard_map(
        on_device,
        mesh=split,
        in_specs=placed,
        out_specs=(P("dp", tps), P("dp"), P("dp")),
        check_vma=False,
    )
```

```python
import jax
import jax.numpy as jnp
from jax import lax
from jax.experimental import pallas as pl
from jax.experimental.pallas import tpu as pltpu
from jax.sharding import Mesh
from jax.sharding import PartitionSpec as P

EXPERT_SLOTS = 4
SUBLANES = 8
LANES = 128
SPLIT = SUBLANES // EXPERT_SLOTS
eps = 1e-06
BF = jnp.bfloat16
F32 = jnp.float32
HIGHEST = lax.Precision.HIGHEST
VMEM = pl.BlockSpec(memory_space=pltpu.VMEM)
SMEM = pl.BlockSpec(memory_space=pltpu.SMEM)
HBM = pl.BlockSpec(memory_space=pltpu.HBM)
MIB = 1 << 20


def dot(a, b, precision=None):
    return jnp.dot(a, b, precision=precision, preferred_element_type=F32)


def iota(shape, axis):
    return lax.broadcasted_iota(jnp.int32, shape, axis)


def shift(x, axis, by):
    n = lax.axis_size(axis)
    return lax.ppermute(x, axis, [(i, (i + by) % n) for i in range(n)])


def stay(*arrays):
    return [pltpu.with_memory_space_constraint(a, pltpu.HBM) for a in arrays]


def early_kernel(his, los, partial_ref, hidden_ref, ids_hbm, prob_hbm, *refs):
    own_ref, held_ref, pick_ref, comb_ref, ids_ref, prob_ref, small, large = refs
    cols = hidden_ref.shape[1]
    l = lax.axis_index("lo")
    first = [
        pltpu.make_async_copy(ids_hbm, ids_ref, small.at[0]),
        pltpu.make_async_copy(prob_hbm, prob_ref, small.at[1]),
    ]
    rest = [pltpu.make_async_copy(hidden_ref, held_ref, large.at[his])]
    for x in range(his):
        at = pl.multiple_of((x * los + l) * cols, LANES)
        rest.append(
            pltpu.make_async_copy(
                partial_ref.at[0, :, pl.ds(at, cols)], own_ref.at[x], large.at[x]
            )
        )
    for copy in first + rest:
        copy.start()
    for copy in first:
        copy.wait()
    names, tokens = ids_ref.shape
    rows, wide = pick_ref.shape[1], comb_ref.shape[2]
    experts = rows // SUBLANES
    ids, prob = ids_ref[...], prob_ref[...].astype(F32)
    expert = iota((experts, tokens), 0)
    match = jnp.zeros((experts, tokens), F32)
    weight = jnp.zeros((experts, tokens), F32)
    for k in range(names):
        same = ids[k : k + 1] == expert
        match = match + jnp.where(same, 1.0, 0.0)
        weight = weight + jnp.where(same, prob[k : k + 1], 0.0)
    earlier = jnp.where(iota((tokens, tokens), 0) < iota((tokens, tokens), 1), 1.0, 0.0)
    slot = jnp.where(match > 0.0, dot(match, earlier, HIGHEST), -1.0)

    def spread(x, count, per):
        owner = jnp.where(iota((count, experts), 0) // per == iota((count, experts), 1), 1.0, 0.0)
        return dot(owner, x, HIGHEST)

    at = iota((rows, tokens), 0)
    slots = spread(slot, rows, SUBLANES)
    for s in range(SPLIT):
        here = (slots == (at % EXPERT_SLOTS).astype(F32)) & (at // EXPERT_SLOTS % SPLIT == s)
        pick_ref[s] = jnp.where(here, 1.0, 0.0).astype(BF)
    at = iota((wide, tokens), 0)
    slots, weights = spread(slot, wide, his * SUBLANES), spread(weight, wide, his * SUBLANES)
    for s in range(SPLIT):
        here = (slots == (at % EXPERT_SLOTS).astype(F32)) & (at // EXPERT_SLOTS % SPLIT == s)
        comb_ref[s] = jnp.where(here, weights, 0.0).T.astype(BF)
    for copy in rest:
        copy.wait()


def choose_kernel(los, pick_ref, own_ref, *refs):
    others, sel_ref, res_ref = refs[: los - 1], refs[los - 1], refs[los]
    his, _, cols = own_ref.shape
    width = cols // SPLIT
    h, l = lax.axis_index("hi"), lax.axis_index("lo")
    for k in range(1, his):
        hh = lax.rem(h + k, his)
        pair = own_ref[hh].astype(F32)
        at = pl.multiple_of((hh * los + l) * cols, LANES)
        for other in others:
            pair = pair + other[:, pl.ds(at, cols)].astype(F32)
        pair = pair.astype(BF)
        res_ref[k - 1] = pair
        chosen = dot(pick_ref[0], pair[:, :width])
        for s in range(1, SPLIT):
            chosen = chosen + dot(pick_ref[s], pair[:, s * width : (s + 1) * width])
        sel_ref[k - 1] = chosen.astype(BF)


def load_kernel(los, *refs):
    hbms, (hidden_ref, pick_ref, own_ref) = refs[:4], refs[4:7]
    others, (mine_ref, sel_ref), sems = refs[7 : 6 + los], refs[10 + los : 12 + los], refs[-1]
    copies = [
        pltpu.make_async_copy(hbm, vmem, sems.at[i])
        for i, (hbm, vmem) in enumerate(zip(hbms, refs[6 + los : 10 + los]))
    ]
    for copy in copies:
        copy.start()
    cols = hidden_ref.shape[1]
    width = cols // SPLIT
    h, l = lax.axis_index("hi"), lax.axis_index("lo")
    mine = hidden_ref[...].astype(F32) + own_ref[h].astype(F32)
    at = pl.multiple_of((h * los + l) * cols, LANES)
    for other in others:
        mine = mine + other[:, pl.ds(at, cols)].astype(F32)
    mine_ref[...] = mine
    chosen = dot(pick_ref[0].astype(F32), mine[:, :width], HIGHEST)
    for s in range(1, SPLIT):
        chosen = chosen + dot(
            pick_ref[s].astype(F32), mine[:, s * width : (s + 1) * width], HIGHEST
        )
    sel_ref[...] = chosen
    for copy in copies:
        copy.wait()


def dispatch_kernel(n, sel_ref, *refs):
    gots, out_ref = refs[:n], refs[n]
    experts, his, subs, width = out_ref.shape
    chosen = sel_ref[...]
    for got in gots:
        chosen = chosen + got[...].astype(F32)
    chosen = chosen.astype(BF).reshape(experts, subs, width)
    for x in range(his):
        out_ref[:, x] = chosen


def regroup(even, odd):
    top = iota(even.shape, 0) < EXPERT_SLOTS
    return (
        jnp.where(top, even, pltpu.roll(odd, EXPERT_SLOTS, 0)),
        jnp.where(top, pltpu.roll(even, EXPERT_SLOTS, 0), odd),
    )


def gather_rows(ref, x, experts):
    his = ref.shape[0] // experts
    low, high = [], []
    for p in range(0, experts, SPLIT):
        even, odd = ref[p * his + x].astype(F32), ref[(p + 1) * his + x].astype(F32)
        first, second = regroup(even, odd)
        low.append(first)
        high.append(second)
    return jnp.concatenate(
        [jnp.concatenate(low, axis=0), jnp.concatenate(high, axis=0)], axis=1
    )


def products(los, helds, gain_ref, wg_ref, wu_ref, gate, up, square, top):
    l, experts = lax.axis_index("lo"), lax.axis_size("dp")
    for k, held in helds:
        his = held.shape[0] // experts
        cols = SPLIT * held.shape[2]
        c = lax.rem(l - k + los, los)
        for x in range(his):
            value = gather_rows(held, x, experts)
            at = pl.multiple_of((x * los + c) * cols, LANES)
            square = square + jnp.sum(value * value, axis=1, keepdims=True)
            value = value * gain_ref[:, pl.ds(at, cols)]
            top = jnp.maximum(top, jnp.max(jnp.abs(value), axis=1, keepdims=True))
            value = value.astype(BF)
            gate = gate + dot(value, wg_ref[0, pl.ds(at, cols), :])
            up = up + dot(value, wu_ref[0, pl.ds(at, cols), :])
    return gate, up, square, top


def first_kernel(los, gain_ref, wg_ref, wu_ref, held_ref, *refs):
    gate_ref, up_ref, square_ref, top_ref = refs
    slots = gate_ref.shape[0]
    zero, none = jnp.zeros(gate_ref.shape, F32), jnp.zeros((slots, 1), F32)
    gate, up, square, top = products(
        los, [(0, held_ref)], gain_ref, wg_ref, wu_ref, zero, zero, none, none
    )
    gate_ref[...] = gate
    up_ref[...] = up
    square_ref[...] = jnp.broadcast_to(square, square_ref.shape)
    top_ref[...] = jnp.broadcast_to(top, top_ref.shape)


def down(act, wd_ref, his, los, c):
    cols = wd_ref.shape[2] // (his * los)
    for x in range(his):
        at = pl.multiple_of((x * los + c) * cols, LANES)
        yield slice(x * cols, (x + 1) * cols), dot(act, wd_ref[0, :, pl.ds(at, cols)])


def second_kernel(his, los, gain_ref, wg_ref, wu_ref, wd_ref, *refs):
    gate_ref, up_ref, square_ref, top_ref = refs[:4]
    helds = refs[4 : 3 + los]
    send_ref, act_ref, peak_ref, out_ref = refs[3 + los :]
    gate, up, square, top = products(
        los,
        list(enumerate(helds, 1)),
        gain_ref,
        wg_ref,
        wu_ref,
        gate_ref[...],
        up_ref[...],
        square_ref[:, :1],
        top_ref[:, :1],
    )
    scale = lax.rsqrt(square / wg_ref.shape[1] + eps)
    out_ref[0] = jnp.max(top * scale).astype(BF).astype(F32)
    gate, up = gate * scale, up * scale
    act = (gate / (1.0 + jnp.exp(-gate)) * up).astype(BF)
    act_ref[...] = act
    peak = jnp.max(jnp.abs(act.astype(F32)))
    peak_ref[...] = jnp.full(peak_ref.shape, peak, F32)
    l, slots = lax.axis_index("lo"), act.shape[0]
    for k in range(1, los):
        for cut, value in down(act, wd_ref, his, los, lax.rem(l + k, los)):
            send_ref[k - 1, :, cut] = value.astype(BF)
        send_ref[k - 1, :, -LANES:] = jnp.full((slots, LANES), peak, F32).astype(BF)


def third_kernel(his, los, act_ref, wd_ref, keep_ref):
    for cut, value in down(act_ref[...], wd_ref, his, los, lax.axis_index("lo")):
        keep_ref[:, cut] = value


def pair_kernel(his, n, keep_ref, peak_ref, *refs):
    gots, out_ref = refs[:n], refs[n]
    blocks, subs, width = out_ref.shape
    width = width - LANES
    cols, experts = SPLIT * width, blocks // his
    peak = jnp.max(peak_ref[...])
    for got in gots:
        peak = jnp.maximum(peak, jnp.max(got[:, -LANES:].astype(F32)))
    for x in range(his):
        total = keep_ref[:, x * cols : (x + 1) * cols]
        for got in gots:
            total = total + got[:, x * cols : (x + 1) * cols].astype(F32)
        for p in range(0, experts, SPLIT):
            rows = slice(p * EXPERT_SLOTS, p * EXPERT_SLOTS + subs)
            even, odd = regroup(total[rows, :width], total[rows, width:])
            out_ref[p * his + x, :, :width] = even.astype(BF)
            out_ref[(p + 1) * his + x, :, :width] = odd.astype(BF)
    out_ref[:, :, width:] = jnp.full((blocks, subs, LANES), peak, F32).astype(BF)


def peak_kernel(his, back_ref, peak_ref):
    peak = back_ref[pl.ds(lax.axis_index("dp") * his, his), :, -LANES:].astype(F32)
    peak_ref[...] = jnp.max(peak, axis=0)


def combine_kernel(mine_ref, comb_ref, back_ref, tile_ref, *refs):
    rests, (out_ref, peak_ref) = refs[:-2], refs[-2:]
    blocks, subs, width = back_ref.shape
    width = width - LANES
    back = back_ref[:, :, :width].reshape(blocks * subs, width)
    for s in range(SPLIT):
        cut = slice(s * width, (s + 1) * width)
        res = mine_ref[:, cut]
        for rest in rests:
            res = res + rest[:, cut].astype(F32)
        out_ref[:, cut] = (res + dot(comb_ref[s], back)).astype(BF)
    peak_ref[0] = jnp.max(tile_ref[...])


def call(kernel, mib, ins, outs, scratch=(), flops=0, moved=0):
    places = [SMEM if isinstance(o, jax.ShapeDtypeStruct) else VMEM for o in outs]
    return pl.pallas_call(
        kernel,
        out_shape=outs,
        in_specs=[HBM if at == "hbm" else VMEM for at, _ in ins],
        out_specs=places,
        scratch_shapes=scratch,
        compiler_params=pltpu.CompilerParams(vmem_limit_bytes=mib * MIB),
        cost_estimate=pl.CostEstimate(flops=flops, bytes_accessed=moved, transcendentals=0),
    )(*[stay(x)[0] if at == "hbm" else x for at, x in ins])


def near(*arrays):
    return [("vmem", a) for a in arrays]


def far(*arrays):
    return [("hbm", a) for a in arrays]


def on_device(attn_partial, hidden_in, norm_gain, expert_ids, route_prob, w_gate, w_up, w_down):
    experts, his, los = lax.axis_size("dp"), lax.axis_size("hi"), lax.axis_size("lo")
    tokens, cols = hidden_in.shape
    _, units = w_gate.shape[1:]
    width, blocks = cols // SPLIT, experts * his
    slots, rows = experts * EXPERT_SLOTS, experts * SUBLANES
    gain = norm_gain.reshape(1, -1)

    others = [shift(attn_partial[0], "lo", k) for k in range(1, los)]
    own, hidden, pick, comb = call(
        lambda *refs: early_kernel(his, los, *refs),
        4,
        far(attn_partial, hidden_in, expert_ids.T, route_prob.T),
        [
            pltpu.VMEM((his, tokens, cols), BF),
            pltpu.VMEM((tokens, cols), BF),
            pltpu.VMEM((SPLIT, rows, tokens), BF),
            pltpu.VMEM((SPLIT, tokens, blocks * SUBLANES), BF),
        ],
        [
            pltpu.VMEM(expert_ids.shape[::-1], expert_ids.dtype),
            pltpu.VMEM(route_prob.shape[::-1], route_prob.dtype),
            pltpu.SemaphoreType.DMA((2,)),
            pltpu.SemaphoreType.DMA((his + 1,)),
        ],
        moved=MIB,
    )
    sels, rests = call(
        lambda *refs: choose_kernel(los, *refs),
        4,
        near(pick, own, *others),
        [
            pltpu.VMEM((his - 1, rows, width), BF),
            pltpu.VMEM((his - 1, tokens, cols), BF),
        ],
    )
    sels = [shift(sels[k - 1], "hi", k) for k in range(1, his)]
    gain, wg, wu, wd, mine, sel = call(
        lambda *refs: load_kernel(los, *refs),
        4,
        far(gain, w_gate, w_up, w_down) + near(hidden, pick, own, *others),
        [
            pltpu.VMEM(gain.shape, F32),
            pltpu.VMEM(w_gate.shape, BF),
            pltpu.VMEM(w_up.shape, BF),
            pltpu.VMEM(w_down.shape, BF),
            pltpu.VMEM((tokens, cols), F32),
            pltpu.VMEM((rows, width), F32),
        ],
        [pltpu.SemaphoreType.DMA((4,))],
        moved=12 * MIB,
    )
    (outgoing,) = call(
        lambda *refs: dispatch_kernel(his - 1, *refs),
        4,
        near(sel, *sels),
        [pltpu.VMEM((experts, his, SUBLANES, width), BF)],
    )
    incoming = lax.all_to_all(
        outgoing.reshape(blocks, SUBLANES, width), ("dp", "hi"), 0, 0, tiled=True
    )
    helds = [shift(incoming, "lo", k) for k in range(1, los)]
    sums = call(
        lambda *refs: first_kernel(los, *refs),
        8,
        near(gain, wg, wu, incoming),
        [
            pltpu.VMEM((slots, units), F32),
            pltpu.VMEM((slots, units), F32),
            pltpu.VMEM((slots, LANES), F32),
            pltpu.VMEM((slots, LANES), F32),
        ],
        moved=4 * MIB,
    )
    sends, act, peak, top = call(
        lambda *refs: second_kernel(his, los, *refs),
        12,
        near(gain, wg, wu, wd, *sums, *helds),
        [
            pltpu.VMEM((los - 1, slots, his * cols + LANES), BF),
            pltpu.VMEM((slots, units), BF),
            pltpu.VMEM((SUBLANES, LANES), F32),
            jax.ShapeDtypeStruct((1,), F32),
        ],
    )
    sends = [shift(sends[k - 1], "lo", k) for k in range(1, los)]
    rests = [shift(rests[k - 1], "hi", k) for k in range(1, his)]
    (keep,) = call(
        lambda *refs: third_kernel(his, los, *refs),
        8,
        near(act, wd),
        [pltpu.VMEM((slots, his * cols), F32)],
        moved=2 * MIB,
    )
    (back,) = call(
        lambda *refs: pair_kernel(his, los - 1, *refs),
        4,
        near(keep, peak, *sends),
        [pltpu.VMEM((blocks, SUBLANES, width + LANES), BF)],
    )
    back = lax.all_to_all(back, ("dp", "hi"), 0, 0, tiled=True)
    (tile,) = call(
        lambda *refs: peak_kernel(his, *refs),
        1,
        near(back),
        [pltpu.VMEM((SUBLANES, LANES), F32)],
    )
    layer_out, hidden_top = pl.pallas_call(
        combine_kernel,
        out_shape=[
            jax.ShapeDtypeStruct((tokens, cols), BF),
            jax.ShapeDtypeStruct((1,), F32),
        ],
        in_specs=[VMEM] * (3 + his),
        out_specs=[VMEM, SMEM],
        compiler_params=pltpu.CompilerParams(vmem_limit_bytes=4 * MIB),
        name="combine",
    )(mine, comb, back, tile, *rests)
    return layer_out, top, hidden_top


def solution(mesh):
    tp = mesh.shape["tp"]
    lo = 2 if tp % 2 == 0 else 1
    split = Mesh(mesh.devices.reshape(mesh.shape["dp"], tp // lo, lo), ("dp", "hi", "lo"))
    tps = ("hi", "lo")
    placed = (
        P(tps, "dp", None),
        P("dp", tps),
        P(),
        P("dp", None),
        P("dp", None),
        P("dp", None, tps),
        P("dp", None, tps),
        P("dp", tps, None),
    )

    return jax.shard_map(
        on_device,
        mesh=split,
        in_specs=placed,
        out_specs=(P("dp", tps), P("dp"), P("dp")),
        check_vma=False,
    )
```

```python
import jax
import jax.numpy as jnp
from jax import lax
from jax.experimental import pallas as pl
from jax.experimental.pallas import tpu as pltpu
from jax.sharding import Mesh
from jax.sharding import PartitionSpec as P

EXPERT_SLOTS = 4
SUBLANES = 8
LANES = 128
SPLIT = SUBLANES // EXPERT_SLOTS
eps = 1e-06
BF = jnp.bfloat16
F32 = jnp.float32
HIGHEST = lax.Precision.HIGHEST
VMEM = pl.BlockSpec(memory_space=pltpu.VMEM)
SMEM = pl.BlockSpec(memory_space=pltpu.SMEM)
HBM = pl.BlockSpec(memory_space=pltpu.HBM)
MIB = 1 << 20


def dot(a, b, precision=None):
    return jnp.dot(a, b, precision=precision, preferred_element_type=F32)


def iota(shape, axis):
    return lax.broadcasted_iota(jnp.int32, shape, axis)


def shift(x, axis, by):
    n = lax.axis_size(axis)
    return lax.ppermute(x, axis, [(i, (i + by) % n) for i in range(n)])


def stay(*arrays):
    return [pltpu.with_memory_space_constraint(a, pltpu.HBM) for a in arrays]


def early_kernel(his, los, partial_ref, hidden_ref, ids_hbm, prob_hbm, *refs):
    own_ref, held_ref, pick_ref, comb_ref, ids_ref, prob_ref, small, large = refs
    cols = hidden_ref.shape[1]
    l = lax.axis_index("lo")
    first = [
        pltpu.make_async_copy(ids_hbm, ids_ref, small.at[0]),
        pltpu.make_async_copy(prob_hbm, prob_ref, small.at[1]),
    ]
    rest = [pltpu.make_async_copy(hidden_ref, held_ref, large.at[his])]
    for x in range(his):
        at = pl.multiple_of((x * los + l) * cols, LANES)
        rest.append(
            pltpu.make_async_copy(
                partial_ref.at[0, :, pl.ds(at, cols)], own_ref.at[x], large.at[x]
            )
        )
    for copy in first + rest:
        copy.start()
    for copy in first:
        copy.wait()
    names, tokens = ids_ref.shape
    rows, wide = pick_ref.shape[1], comb_ref.shape[2]
    experts = rows // SUBLANES
    ids, prob = ids_ref[...], prob_ref[...].astype(F32)
    expert = iota((experts, tokens), 0)
    match = jnp.zeros((experts, tokens), F32)
    weight = jnp.zeros((experts, tokens), F32)
    for k in range(names):
        same = ids[k : k + 1] == expert
        match = match + jnp.where(same, 1.0, 0.0)
        weight = weight + jnp.where(same, prob[k : k + 1], 0.0)
    earlier = jnp.where(iota((tokens, tokens), 0) < iota((tokens, tokens), 1), 1.0, 0.0)
    slot = jnp.where(match > 0.0, dot(match, earlier, HIGHEST), -1.0)

    def spread(x, count, per):
        owner = jnp.where(iota((count, experts), 0) // per == iota((count, experts), 1), 1.0, 0.0)
        return dot(owner, x, HIGHEST)

    at = iota((rows, tokens), 0)
    slots = spread(slot, rows, SUBLANES)
    for s in range(SPLIT):
        here = (slots == (at % EXPERT_SLOTS).astype(F32)) & (at // EXPERT_SLOTS % SPLIT == s)
        pick_ref[s] = jnp.where(here, 1.0, 0.0).astype(BF)
    at = iota((wide, tokens), 0)
    slots, weights = spread(slot, wide, his * SUBLANES), spread(weight, wide, his * SUBLANES)
    for s in range(SPLIT):
        here = (slots == (at % EXPERT_SLOTS).astype(F32)) & (at // EXPERT_SLOTS % SPLIT == s)
        comb_ref[s] = jnp.where(here, weights, 0.0).T.astype(BF)
    for copy in rest:
        copy.wait()


def choose_kernel(los, pick_ref, own_ref, *refs):
    others, sel_ref, res_ref = refs[: los - 1], refs[los - 1], refs[los]
    his, _, cols = own_ref.shape
    width = cols // SPLIT
    h, l = lax.axis_index("hi"), lax.axis_index("lo")
    for k in range(1, his):
        hh = lax.rem(h + k, his)
        pair = own_ref[hh].astype(F32)
        at = pl.multiple_of((hh * los + l) * cols, LANES)
        for other in others:
            pair = pair + other[:, pl.ds(at, cols)].astype(F32)
        pair = pair.astype(BF)
        res_ref[k - 1] = pair
        chosen = dot(pick_ref[0], pair[:, :width])
        for s in range(1, SPLIT):
            chosen = chosen + dot(pick_ref[s], pair[:, s * width : (s + 1) * width])
        sel_ref[k - 1] = chosen.astype(BF)


def load_kernel(los, *refs):
    hbms, (hidden_ref, pick_ref, own_ref) = refs[:4], refs[4:7]
    others, (mine_ref, sel_ref), sems = refs[7 : 6 + los], refs[10 + los : 12 + los], refs[-1]
    copies = [
        pltpu.make_async_copy(hbm, vmem, sems.at[i])
        for i, (hbm, vmem) in enumerate(zip(hbms, refs[6 + los : 10 + los]))
    ]
    for copy in copies:
        copy.start()
    cols = hidden_ref.shape[1]
    width = cols // SPLIT
    h, l = lax.axis_index("hi"), lax.axis_index("lo")
    mine = hidden_ref[...].astype(F32) + own_ref[h].astype(F32)
    at = pl.multiple_of((h * los + l) * cols, LANES)
    for other in others:
        mine = mine + other[:, pl.ds(at, cols)].astype(F32)
    mine_ref[...] = mine
    chosen = dot(pick_ref[0].astype(F32), mine[:, :width], HIGHEST)
    for s in range(1, SPLIT):
        chosen = chosen + dot(
            pick_ref[s].astype(F32), mine[:, s * width : (s + 1) * width], HIGHEST
        )
    sel_ref[...] = chosen
    for copy in copies:
        copy.wait()


def dispatch_kernel(n, sel_ref, *refs):
    gots, out_ref = refs[:n], refs[n]
    experts, his, subs, width = out_ref.shape
    chosen = sel_ref[...]
    for got in gots:
        chosen = chosen + got[...].astype(F32)
    chosen = chosen.astype(BF).reshape(experts, subs, width)
    for x in range(his):
        out_ref[:, x] = chosen


def regroup(even, odd):
    top = iota(even.shape, 0) < EXPERT_SLOTS
    return (
        jnp.where(top, even, pltpu.roll(odd, EXPERT_SLOTS, 0)),
        jnp.where(top, pltpu.roll(even, EXPERT_SLOTS, 0), odd),
    )


def gather_rows(ref, x, experts):
    his = ref.shape[0] // experts
    low, high = [], []
    for p in range(0, experts, SPLIT):
        even, odd = ref[p * his + x].astype(F32), ref[(p + 1) * his + x].astype(F32)
        first, second = regroup(even, odd)
        low.append(first)
        high.append(second)
    return jnp.concatenate(
        [jnp.concatenate(low, axis=0), jnp.concatenate(high, axis=0)], axis=1
    )


def products(los, helds, gain_ref, wg_ref, wu_ref, gate, up, square, top):
    l, experts = lax.axis_index("lo"), lax.axis_size("dp")
    for k, held in helds:
        his = held.shape[0] // experts
        cols = SPLIT * held.shape[2]
        c = lax.rem(l - k + los, los)
        for x in range(his):
            value = gather_rows(held, x, experts)
            at = pl.multiple_of((x * los + c) * cols, LANES)
            square = square + jnp.sum(value * value, axis=1, keepdims=True)
            value = value * gain_ref[:, pl.ds(at, cols)]
            top = jnp.maximum(top, jnp.max(jnp.abs(value), axis=1, keepdims=True))
            value = value.astype(BF)
            gate = gate + dot(value, wg_ref[0, pl.ds(at, cols), :])
            up = up + dot(value, wu_ref[0, pl.ds(at, cols), :])
    return gate, up, square, top


def first_kernel(los, gain_ref, wg_ref, wu_ref, held_ref, *refs):
    gate_ref, up_ref, square_ref, top_ref = refs
    slots = gate_ref.shape[0]
    zero, none = jnp.zeros(gate_ref.shape, F32), jnp.zeros((slots, 1), F32)
    gate, up, square, top = products(
        los, [(0, held_ref)], gain_ref, wg_ref, wu_ref, zero, zero, none, none
    )
    gate_ref[...] = gate
    up_ref[...] = up
    square_ref[...] = jnp.broadcast_to(square, square_ref.shape)
    top_ref[...] = jnp.broadcast_to(top, top_ref.shape)


def down(act, wd_ref, his, los, c):
    cols = wd_ref.shape[2] // (his * los)
    for x in range(his):
        at = pl.multiple_of((x * los + c) * cols, LANES)
        yield slice(x * cols, (x + 1) * cols), dot(act, wd_ref[0, :, pl.ds(at, cols)])


def second_kernel(los, gain_ref, wg_ref, wu_ref, *refs):
    gate_ref, up_ref, square_ref, top_ref = refs[:4]
    helds = refs[4 : 3 + los]
    act_ref, peak_ref, out_ref = refs[3 + los :]
    gate, up, square, top = products(
        los,
        list(enumerate(helds, 1)),
        gain_ref,
        wg_ref,
        wu_ref,
        gate_ref[...],
        up_ref[...],
        square_ref[:, :1],
        top_ref[:, :1],
    )
    scale = lax.rsqrt(square / wg_ref.shape[1] + eps)
    out_ref[...] = jnp.full(out_ref.shape, jnp.max(top * scale), F32)
    gate, up = gate * scale, up * scale
    act = (gate / (1.0 + jnp.exp(-gate)) * up).astype(BF)
    act_ref[...] = act
    peak = jnp.max(jnp.abs(act.astype(F32)))
    peak_ref[...] = jnp.full(peak_ref.shape, peak, F32)


def down_kernel(his, los, act_ref, wd_ref, send_ref):
    for k in range(1, los):
        c = lax.rem(lax.axis_index("lo") + k, los)
        for cut, value in down(act_ref[...], wd_ref, his, los, c):
            send_ref[k - 1, :, cut] = value.astype(BF)


def third_kernel(his, los, act_ref, wd_ref, keep_ref):
    for cut, value in down(act_ref[...], wd_ref, his, los, lax.axis_index("lo")):
        keep_ref[:, cut] = value


def tag_kernel(los, rests_ref, peak_ref, *refs):
    tiles, (out_ref, tile_ref) = refs[: los - 1], refs[los - 1 :]
    peak = peak_ref[...]
    for tile in tiles:
        peak = jnp.maximum(peak, tile[...])
    tile_ref[...] = peak
    cols = rests_ref.shape[2]
    for k in range(rests_ref.shape[0]):
        out_ref[k, :, :cols] = rests_ref[k]
        out_ref[k, :, cols:] = jnp.broadcast_to(peak[:1], (out_ref.shape[1], LANES)).astype(BF)


def pair_kernel(his, n, keep_ref, *refs):
    gots, out_ref = refs[:n], refs[n]
    blocks, subs, width = out_ref.shape
    cols, experts = SPLIT * width, blocks // his
    for x in range(his):
        total = keep_ref[:, x * cols : (x + 1) * cols]
        for got in gots:
            total = total + got[:, x * cols : (x + 1) * cols].astype(F32)
        for p in range(0, experts, SPLIT):
            rows = slice(p * EXPERT_SLOTS, p * EXPERT_SLOTS + subs)
            even, odd = regroup(total[rows, :width], total[rows, width:])
            out_ref[p * his + x, :, :width] = even.astype(BF)
            out_ref[(p + 1) * his + x, :, :width] = odd.astype(BF)


def hold_kernel(back_ref, tile_ref, out_ref):
    out_ref[...] = tile_ref[...]


def combine_kernel(his, mine_ref, comb_ref, back_ref, top_ref, tile_ref, *refs):
    rests, (out_ref, input_ref, hidden_ref) = refs[: his - 1], refs[-3:]
    input_ref[0] = jnp.max(top_ref[...].astype(BF).astype(F32))
    blocks, subs, width = back_ref.shape
    back = back_ref[...].reshape(blocks * subs, width)
    for s in range(SPLIT):
        cut = slice(s * width, (s + 1) * width)
        res = mine_ref[:, cut]
        for rest in rests:
            res = res + rest[:, cut].astype(F32)
        out_ref[:, cut] = (res + dot(comb_ref[s], back)).astype(BF)
    peak = tile_ref[...]
    for rest in rests:
        peak = jnp.maximum(peak, rest[:SUBLANES, -LANES:].astype(F32))
    hidden_ref[0] = jnp.max(peak)


def call(kernel, mib, ins, outs, scratch=(), flops=0, moved=0):
    places = [SMEM if isinstance(o, jax.ShapeDtypeStruct) else VMEM for o in outs]
    return pl.pallas_call(
        kernel,
        out_shape=outs,
        in_specs=[HBM if at == "hbm" else VMEM for at, _ in ins],
        out_specs=places,
        scratch_shapes=scratch,
        compiler_params=pltpu.CompilerParams(vmem_limit_bytes=mib * MIB),
        cost_estimate=pl.CostEstimate(flops=flops, bytes_accessed=moved, transcendentals=0),
    )(*[stay(x)[0] if at == "hbm" else x for at, x in ins])


def near(*arrays):
    return [("vmem", a) for a in arrays]


def far(*arrays):
    return [("hbm", a) for a in arrays]


def on_device(attn_partial, hidden_in, norm_gain, expert_ids, route_prob, w_gate, w_up, w_down):
    experts, his, los = lax.axis_size("dp"), lax.axis_size("hi"), lax.axis_size("lo")
    tokens, cols = hidden_in.shape
    _, units = w_gate.shape[1:]
    width, blocks = cols // SPLIT, experts * his
    slots, rows = experts * EXPERT_SLOTS, experts * SUBLANES
    gain = norm_gain.reshape(1, -1)

    others = [shift(attn_partial[0], "lo", k) for k in range(1, los)]
    own, hidden, pick, comb = call(
        lambda *refs: early_kernel(his, los, *refs),
        4,
        far(attn_partial, hidden_in, expert_ids.T, route_prob.T),
        [
            pltpu.VMEM((his, tokens, cols), BF),
            pltpu.VMEM((tokens, cols), BF),
            pltpu.VMEM((SPLIT, rows, tokens), BF),
            pltpu.VMEM((SPLIT, tokens, blocks * SUBLANES), BF),
        ],
        [
            pltpu.VMEM(expert_ids.shape[::-1], expert_ids.dtype),
            pltpu.VMEM(route_prob.shape[::-1], route_prob.dtype),
            pltpu.SemaphoreType.DMA((2,)),
            pltpu.SemaphoreType.DMA((his + 1,)),
        ],
        moved=MIB,
    )
    sels, rests = call(
        lambda *refs: choose_kernel(los, *refs),
        4,
        near(pick, own, *others),
        [
            pltpu.VMEM((his - 1, rows, width), BF),
            pltpu.VMEM((his - 1, tokens, cols), BF),
        ],
    )
    sels = [shift(sels[k - 1], "hi", k) for k in range(1, his)]
    gain, wg, wu, wd, mine, sel = call(
        lambda *refs: load_kernel(los, *refs),
        4,
        far(gain, w_gate, w_up, w_down) + near(hidden, pick, own, *others),
        [
            pltpu.VMEM(gain.shape, F32),
            pltpu.VMEM(w_gate.shape, BF),
            pltpu.VMEM(w_up.shape, BF),
            pltpu.VMEM(w_down.shape, BF),
            pltpu.VMEM((tokens, cols), F32),
            pltpu.VMEM((rows, width), F32),
        ],
        [pltpu.SemaphoreType.DMA((4,))],
        moved=12 * MIB,
    )
    (outgoing,) = call(
        lambda *refs: dispatch_kernel(his - 1, *refs),
        4,
        near(sel, *sels),
        [pltpu.VMEM((experts, his, SUBLANES, width), BF)],
    )
    incoming = lax.all_to_all(
        outgoing.reshape(blocks, SUBLANES, width), ("dp", "hi"), 0, 0, tiled=True
    )
    helds = [shift(incoming, "lo", k) for k in range(1, los)]
    sums = call(
        lambda *refs: first_kernel(los, *refs),
        8,
        near(gain, wg, wu, incoming),
        [
            pltpu.VMEM((slots, units), F32),
            pltpu.VMEM((slots, units), F32),
            pltpu.VMEM((slots, LANES), F32),
            pltpu.VMEM((slots, LANES), F32),
        ],
        moved=4 * MIB,
    )
    act, peak, top = call(
        lambda *refs: second_kernel(los, *refs),
        8,
        near(gain, wg, wu, *sums, *helds),
        [
            pltpu.VMEM((slots, units), BF),
            pltpu.VMEM((SUBLANES, LANES), F32),
            pltpu.VMEM((SUBLANES, LANES), F32),
        ],
    )
    tiles = [shift(peak, "lo", k) for k in range(1, los)]
    (sends,) = call(
        lambda *refs: down_kernel(his, los, *refs),
        8,
        near(act, wd),
        [pltpu.VMEM((los - 1, slots, his * cols), BF)],
        moved=2 * MIB,
    )
    sends = [shift(sends[k - 1], "lo", k) for k in range(1, los)]
    (keep,) = call(
        lambda *refs: third_kernel(his, los, *refs),
        8,
        near(act, wd),
        [pltpu.VMEM((slots, his * cols), F32)],
        moved=2 * MIB,
    )
    rests, tile = call(
        lambda *refs: tag_kernel(los, *refs),
        4,
        near(rests, peak, *tiles),
        [
            pltpu.VMEM((his - 1, tokens, cols + LANES), BF),
            pltpu.VMEM((SUBLANES, LANES), F32),
        ],
    )
    rests = [shift(rests[k - 1], "hi", k) for k in range(1, his)]
    (back,) = call(
        lambda *refs: pair_kernel(his, los - 1, *refs),
        4,
        near(keep, *sends),
        [pltpu.VMEM((blocks, SUBLANES, width), BF)],
    )
    back = lax.all_to_all(back, ("dp", "hi"), 0, 0, tiled=True)
    (tile,) = call(hold_kernel, 1, near(back, tile), [pltpu.VMEM((SUBLANES, LANES), F32)])
    layer_out, input_top, hidden_top = pl.pallas_call(
        lambda *refs: combine_kernel(his, *refs),
        out_shape=[
            jax.ShapeDtypeStruct((tokens, cols), BF),
            jax.ShapeDtypeStruct((1,), F32),
            jax.ShapeDtypeStruct((1,), F32),
        ],
        in_specs=[VMEM] * (4 + his),
        out_specs=[VMEM, SMEM, SMEM],
        compiler_params=pltpu.CompilerParams(vmem_limit_bytes=4 * MIB),
        name="combine",
    )(mine, comb, back, top, tile, *rests)
    return layer_out, input_top, hidden_top


def solution(mesh):
    tp = mesh.shape["tp"]
    lo = 2 if tp % 2 == 0 else 1
    split = Mesh(mesh.devices.reshape(mesh.shape["dp"], tp // lo, lo), ("dp", "hi", "lo"))
    tps = ("hi", "lo")
    placed = (
        P(tps, "dp", None),
        P("dp", tps),
        P(),
        P("dp", None),
        P("dp", None),
        P("dp", None, tps),
        P("dp", None, tps),
        P("dp", tps, None),
    )

    return jax.shard_map(
        on_device,
        mesh=split,
        in_specs=placed,
        out_specs=(P("dp", tps), P("dp"), P("dp")),
        check_vma=False,
    )
```

```python
import jax
import jax.numpy as jnp
from jax import lax
from jax.experimental import pallas as pl
from jax.experimental.pallas import tpu as pltpu
from jax.sharding import Mesh
from jax.sharding import PartitionSpec as P

EXPERT_SLOTS = 4
SUBLANES = 8
LANES = 128
SPLIT = SUBLANES // EXPERT_SLOTS
eps = 1e-06
BF = jnp.bfloat16
F32 = jnp.float32
HIGHEST = lax.Precision.HIGHEST
VMEM = pl.BlockSpec(memory_space=pltpu.VMEM)
SMEM = pl.BlockSpec(memory_space=pltpu.SMEM)
HBM = pl.BlockSpec(memory_space=pltpu.HBM)
MIB = 1 << 20


def dot(a, b, precision=None):
    return jnp.dot(a, b, precision=precision, preferred_element_type=F32)


def iota(shape, axis):
    return lax.broadcasted_iota(jnp.int32, shape, axis)


def shift(x, axis, by):
    n = lax.axis_size(axis)
    return lax.ppermute(x, axis, [(i, (i + by) % n) for i in range(n)])


def stay(*arrays):
    return [pltpu.with_memory_space_constraint(a, pltpu.HBM) for a in arrays]


def early_kernel(his, los, partial_ref, hidden_ref, ids_hbm, prob_hbm, *refs):
    own_ref, held_ref, pick_ref, comb_ref, ids_ref, prob_ref, small, large = refs
    cols = hidden_ref.shape[1]
    l = lax.axis_index("lo")
    first = [
        pltpu.make_async_copy(ids_hbm, ids_ref, small.at[0]),
        pltpu.make_async_copy(prob_hbm, prob_ref, small.at[1]),
    ]
    rest = [pltpu.make_async_copy(hidden_ref, held_ref, large.at[his])]
    for x in range(his):
        at = pl.multiple_of((x * los + l) * cols, LANES)
        rest.append(
            pltpu.make_async_copy(
                partial_ref.at[0, :, pl.ds(at, cols)], own_ref.at[x], large.at[x]
            )
        )
    for copy in first + rest:
        copy.start()
    for copy in first:
        copy.wait()
    names, tokens = ids_ref.shape
    rows, wide = pick_ref.shape[1], comb_ref.shape[1]
    experts = rows // SUBLANES
    ids, prob = ids_ref[...], prob_ref[...].astype(F32)
    expert = iota((experts, tokens), 0)
    match = jnp.zeros((experts, tokens), F32)
    weight = jnp.zeros((experts, tokens), F32)
    for k in range(names):
        same = ids[k : k + 1] == expert
        match = match + jnp.where(same, 1.0, 0.0)
        weight = weight + jnp.where(same, prob[k : k + 1], 0.0)
    earlier = jnp.where(iota((tokens, tokens), 0) < iota((tokens, tokens), 1), 1.0, 0.0)
    slot = jnp.where(match > 0.0, dot(match, earlier, HIGHEST), -1.0)

    def spread(x, count, per):
        owner = jnp.where(iota((count, experts), 0) // per == iota((count, experts), 1), 1.0, 0.0)
        return dot(owner, x, HIGHEST)

    at = iota((rows, tokens), 0)
    slots = spread(slot, rows, SUBLANES)
    for s in range(SPLIT):
        here = (slots == (at % EXPERT_SLOTS).astype(F32)) & (at // EXPERT_SLOTS % SPLIT == s)
        pick_ref[s] = jnp.where(here, 1.0, 0.0).astype(BF)
    at = iota((wide, tokens), 0)
    per = his * EXPERT_SLOTS
    slots, weights = spread(slot, wide, per), spread(weight, wide, per)
    here = slots == (at % EXPERT_SLOTS).astype(F32)
    comb_ref[...] = jnp.where(here, weights, 0.0).T.astype(BF)
    for copy in rest:
        copy.wait()


def choose_kernel(los, pick_ref, own_ref, *refs):
    others, sel_ref, res_ref = refs[: los - 1], refs[los - 1], refs[los]
    his, _, cols = own_ref.shape
    width = cols // SPLIT
    h, l = lax.axis_index("hi"), lax.axis_index("lo")
    for k in range(1, his):
        hh = lax.rem(h + k, his)
        pair = own_ref[hh].astype(F32)
        at = pl.multiple_of((hh * los + l) * cols, LANES)
        for other in others:
            pair = pair + other[:, pl.ds(at, cols)].astype(F32)
        pair = pair.astype(BF)
        res_ref[k - 1] = pair
        chosen = dot(pick_ref[0], pair[:, :width])
        for s in range(1, SPLIT):
            chosen = chosen + dot(pick_ref[s], pair[:, s * width : (s + 1) * width])
        sel_ref[k - 1] = chosen.astype(BF)


def load_kernel(los, *refs):
    hbms, (hidden_ref, pick_ref, own_ref) = refs[:4], refs[4:7]
    others, (mine_ref, sel_ref), sems = refs[7 : 6 + los], refs[10 + los : 12 + los], refs[-1]
    copies = [
        pltpu.make_async_copy(hbm, vmem, sems.at[i])
        for i, (hbm, vmem) in enumerate(zip(hbms, refs[6 + los : 10 + los]))
    ]
    for copy in copies:
        copy.start()
    cols = hidden_ref.shape[1]
    width = cols // SPLIT
    h, l = lax.axis_index("hi"), lax.axis_index("lo")
    mine = hidden_ref[...].astype(F32) + own_ref[h].astype(F32)
    at = pl.multiple_of((h * los + l) * cols, LANES)
    for other in others:
        mine = mine + other[:, pl.ds(at, cols)].astype(F32)
    mine_ref[...] = mine
    chosen = dot(pick_ref[0].astype(F32), mine[:, :width], HIGHEST)
    for s in range(1, SPLIT):
        chosen = chosen + dot(
            pick_ref[s].astype(F32), mine[:, s * width : (s + 1) * width], HIGHEST
        )
    sel_ref[...] = chosen
    for copy in copies:
        copy.wait()


def dispatch_kernel(n, sel_ref, *refs):
    gots, out_ref = refs[:n], refs[n]
    experts, his, subs, width = out_ref.shape
    chosen = sel_ref[...]
    for got in gots:
        chosen = chosen + got[...].astype(F32)
    chosen = chosen.astype(BF).reshape(experts, subs, width)
    for x in range(his):
        out_ref[:, x] = chosen


def regroup(even, odd):
    top = iota(even.shape, 0) < EXPERT_SLOTS
    return (
        jnp.where(top, even, pltpu.roll(odd, EXPERT_SLOTS, 0)),
        jnp.where(top, pltpu.roll(even, EXPERT_SLOTS, 0), odd),
    )


def gather_rows(ref, x, experts):
    his = ref.shape[0] // experts
    low, high = [], []
    for p in range(0, experts, SPLIT):
        even, odd = ref[p * his + x].astype(F32), ref[(p + 1) * his + x].astype(F32)
        first, second = regroup(even, odd)
        low.append(first)
        high.append(second)
    return jnp.concatenate(
        [jnp.concatenate(low, axis=0), jnp.concatenate(high, axis=0)], axis=1
    )


def products(los, helds, gain_ref, wg_ref, wu_ref, gate, up, square, top):
    l, experts = lax.axis_index("lo"), lax.axis_size("dp")
    for k, held in helds:
        his = held.shape[0] // experts
        cols = SPLIT * held.shape[2]
        c = lax.rem(l - k + los, los)
        for x in range(his):
            value = gather_rows(held, x, experts)
            at = pl.multiple_of((x * los + c) * cols, LANES)
            square = square + jnp.sum(value * value, axis=1, keepdims=True)
            value = value * gain_ref[:, pl.ds(at, cols)]
            top = jnp.maximum(top, jnp.max(jnp.abs(value), axis=1, keepdims=True))
            value = value.astype(BF)
            for n in range(0, cols, 896):
                part, here = value[:, n : n + 896], pl.ds(at + n, 896)
                gate = gate + dot(part, wg_ref[0, here, :])
                up = up + dot(part, wu_ref[0, here, :])
    return gate, up, square, top


def first_kernel(los, gain_ref, wg_ref, wu_ref, held_ref, *refs):
    gate_ref, up_ref, square_ref, top_ref = refs
    slots = gate_ref.shape[0]
    zero, none = jnp.zeros(gate_ref.shape, F32), jnp.zeros((slots, 1), F32)
    gate, up, square, top = products(
        los, [(0, held_ref)], gain_ref, wg_ref, wu_ref, zero, zero, none, none
    )
    gate_ref[...] = gate
    up_ref[...] = up
    square_ref[...] = jnp.broadcast_to(square, square_ref.shape)
    top_ref[...] = jnp.broadcast_to(top, top_ref.shape)


def down(act, wd_ref, his, los, c):
    cols = wd_ref.shape[2] // (his * los)
    for x in range(his):
        at = pl.multiple_of((x * los + c) * cols, LANES)
        yield slice(x * cols, (x + 1) * cols), dot(act, wd_ref[0, :, pl.ds(at, cols)])


def second_kernel(his, los, gain_ref, wg_ref, wu_ref, wd_ref, *refs):
    gate_ref, up_ref, square_ref, top_ref = refs[:4]
    helds = refs[4 : 3 + los]
    send_ref, act_ref, peak_ref, out_ref = refs[3 + los :]
    gate, up, square, top = products(
        los,
        list(enumerate(helds, 1)),
        gain_ref,
        wg_ref,
        wu_ref,
        gate_ref[...],
        up_ref[...],
        square_ref[:, :1],
        top_ref[:, :1],
    )
    scale = lax.rsqrt(square / wg_ref.shape[1] + eps)
    out_ref[...] = jnp.full(out_ref.shape, jnp.max(top * scale), F32)
    gate, up = gate * scale, up * scale
    act = (gate / (1.0 + jnp.exp(-gate)) * up).astype(BF)
    act_ref[...] = act
    peak = jnp.max(jnp.abs(act.astype(F32)))
    peak_ref[...] = jnp.full(peak_ref.shape, peak, F32)
    for k in range(1, los):
        c = lax.rem(lax.axis_index("lo") + k, los)
        for cut, value in down(act, wd_ref, his, los, c):
            send_ref[k - 1, :, cut] = value.astype(BF)
        send_ref[k - 1, :, -LANES:] = jnp.full((act.shape[0], LANES), peak, F32).astype(BF)


def third_kernel(his, los, act_ref, wd_ref, keep_ref):
    for cut, value in down(act_ref[...], wd_ref, his, los, lax.axis_index("lo")):
        keep_ref[:, cut] = value


def pair_kernel(his, n, keep_ref, peak_ref, *refs):
    gots, out_ref = refs[:n], refs[n]
    experts, cols = out_ref.shape[0] // his, out_ref.shape[2] - LANES
    peak = peak_ref[:EXPERT_SLOTS]
    for got in gots:
        peak = jnp.maximum(peak, got[:EXPERT_SLOTS, -LANES:].astype(F32))
    for x in range(his):
        total = keep_ref[:, x * cols : (x + 1) * cols]
        for got in gots:
            total = total + got[:, x * cols : (x + 1) * cols].astype(F32)
        for e in range(experts):
            rows = total[e * EXPERT_SLOTS : (e + 1) * EXPERT_SLOTS]
            out_ref[e * his + x, :, :cols] = rows.astype(BF)
            out_ref[e * his + x, :, cols:] = peak.astype(BF)


def hold_kernel(his, back_ref, out_ref):
    peak = back_ref[pl.ds(lax.axis_index("dp") * his, his), :, -LANES:].astype(F32)
    out_ref[...] = jnp.max(peak, axis=0)


def combine_kernel(his, mine_ref, comb_ref, back_ref, top_ref, tile_ref, *refs):
    rests, (out_ref, input_ref, hidden_ref) = refs[: his - 1], refs[-3:]
    input_ref[0] = jnp.max(top_ref[...].astype(BF).astype(F32))
    hidden_ref[0] = jnp.max(tile_ref[...])
    blocks, slots, cols = back_ref.shape
    cols = cols - LANES
    back = back_ref[:, :, :cols].reshape(blocks * slots, cols)
    res = mine_ref[...]
    for rest in rests:
        res = res + rest[...].astype(F32)
    out_ref[...] = (res + dot(comb_ref[...], back)).astype(BF)


def call(kernel, mib, ins, outs, scratch=(), flops=0, moved=0):
    places = [SMEM if isinstance(o, jax.ShapeDtypeStruct) else VMEM for o in outs]
    return pl.pallas_call(
        kernel,
        out_shape=outs,
        in_specs=[HBM if at == "hbm" else VMEM for at, _ in ins],
        out_specs=places,
        scratch_shapes=scratch,
        compiler_params=pltpu.CompilerParams(vmem_limit_bytes=mib * MIB),
        cost_estimate=pl.CostEstimate(flops=flops, bytes_accessed=moved, transcendentals=0),
    )(*[stay(x)[0] if at == "hbm" else x for at, x in ins])


def near(*arrays):
    return [("vmem", a) for a in arrays]


def far(*arrays):
    return [("hbm", a) for a in arrays]


def on_device(attn_partial, hidden_in, norm_gain, expert_ids, route_prob, w_gate, w_up, w_down):
    experts, his, los = lax.axis_size("dp"), lax.axis_size("hi"), lax.axis_size("lo")
    tokens, cols = hidden_in.shape
    _, units = w_gate.shape[1:]
    width, blocks = cols // SPLIT, experts * his
    slots, rows = experts * EXPERT_SLOTS, experts * SUBLANES
    gain = norm_gain.reshape(1, -1)

    others = [shift(attn_partial[0], "lo", k) for k in range(1, los)]
    own, hidden, pick, comb = call(
        lambda *refs: early_kernel(his, los, *refs),
        4,
        far(attn_partial, hidden_in, expert_ids.T, route_prob.T),
        [
            pltpu.VMEM((his, tokens, cols), BF),
            pltpu.VMEM((tokens, cols), BF),
            pltpu.VMEM((SPLIT, rows, tokens), BF),
            pltpu.VMEM((tokens, blocks * EXPERT_SLOTS), BF),
        ],
        [
            pltpu.VMEM(expert_ids.shape[::-1], expert_ids.dtype),
            pltpu.VMEM(route_prob.shape[::-1], route_prob.dtype),
            pltpu.SemaphoreType.DMA((2,)),
            pltpu.SemaphoreType.DMA((his + 1,)),
        ],
        moved=MIB,
    )
    sels, rests = call(
        lambda *refs: choose_kernel(los, *refs),
        4,
        near(pick, own, *others),
        [
            pltpu.VMEM((his - 1, rows, width), BF),
            pltpu.VMEM((his - 1, tokens, cols), BF),
        ],
    )
    sels = [shift(sels[k - 1], "hi", k) for k in range(1, his)]
    gain, wg, wu, wd, mine, sel = call(
        lambda *refs: load_kernel(los, *refs),
        4,
        far(gain, w_gate, w_up, w_down) + near(hidden, pick, own, *others),
        [
            pltpu.VMEM(gain.shape, F32),
            pltpu.VMEM(w_gate.shape, BF),
            pltpu.VMEM(w_up.shape, BF),
            pltpu.VMEM(w_down.shape, BF),
            pltpu.VMEM((tokens, cols), F32),
            pltpu.VMEM((rows, width), F32),
        ],
        [pltpu.SemaphoreType.DMA((4,))],
        moved=12 * MIB,
    )
    (outgoing,) = call(
        lambda *refs: dispatch_kernel(his - 1, *refs),
        4,
        near(sel, *sels),
        [pltpu.VMEM((experts, his, SUBLANES, width), BF)],
    )
    incoming = lax.all_to_all(
        outgoing.reshape(blocks, SUBLANES, width), ("dp", "hi"), 0, 0, tiled=True
    )
    helds = [shift(incoming, "lo", k) for k in range(1, los)]
    rests = [shift(rests[k - 1], "hi", k) for k in range(1, his)]
    sums = call(
        lambda *refs: first_kernel(los, *refs),
        8,
        near(gain, wg, wu, incoming),
        [
            pltpu.VMEM((slots, units), F32),
            pltpu.VMEM((slots, units), F32),
            pltpu.VMEM((slots, LANES), F32),
            pltpu.VMEM((slots, LANES), F32),
        ],
        moved=4 * MIB,
    )
    sends, act, peak, top = call(
        lambda *refs: second_kernel(his, los, *refs),
        8,
        near(gain, wg, wu, wd, *sums, *helds),
        [
            pltpu.VMEM((los - 1, slots, his * cols + LANES), BF),
            pltpu.VMEM((slots, units), BF),
            pltpu.VMEM((SUBLANES, LANES), F32),
            pltpu.VMEM((SUBLANES, LANES), F32),
        ],
    )
    sends = [shift(sends[k - 1], "lo", k) for k in range(1, los)]
    (keep,) = call(
        lambda *refs: third_kernel(his, los, *refs),
        8,
        near(act, wd),
        [pltpu.VMEM((slots, his * cols), F32)],
        moved=2 * MIB,
    )
    (back,) = call(
        lambda *refs: pair_kernel(his, los - 1, *refs),
        4,
        near(keep, peak, *sends),
        [pltpu.VMEM((blocks, EXPERT_SLOTS, cols + LANES), BF)],
    )
    back = lax.all_to_all(back, ("dp", "hi"), 0, 0, tiled=True)
    (tile,) = call(
        lambda *refs: hold_kernel(his, *refs),
        1,
        near(back),
        [pltpu.VMEM((EXPERT_SLOTS, LANES), F32)],
    )
    layer_out, input_top, hidden_top = pl.pallas_call(
        lambda *refs: combine_kernel(his, *refs),
        out_shape=[
            jax.ShapeDtypeStruct((tokens, cols), BF),
            jax.ShapeDtypeStruct((1,), F32),
            jax.ShapeDtypeStruct((1,), F32),
        ],
        in_specs=[VMEM] * (4 + his),
        out_specs=[VMEM, SMEM, SMEM],
        compiler_params=pltpu.CompilerParams(vmem_limit_bytes=4 * MIB),
        name="combine",
    )(mine, comb, back, top, tile, *rests)
    return layer_out, input_top, hidden_top


def solution(mesh):
    tp = mesh.shape["tp"]
    lo = 2 if tp % 2 == 0 else 1
    split = Mesh(mesh.devices.reshape(mesh.shape["dp"], tp // lo, lo), ("dp", "hi", "lo"))
    tps = ("hi", "lo")
    placed = (
        P(tps, "dp", None),
        P("dp", tps),
        P(),
        P("dp", None),
        P("dp", None),
        P("dp", None, tps),
        P("dp", None, tps),
        P("dp", tps, None),
    )

    return jax.shard_map(
        on_device,
        mesh=split,
        in_specs=placed,
        out_specs=(P("dp", tps), P("dp"), P("dp")),
        check_vma=False,
    )
```

```python
import jax
import jax.numpy as jnp
from jax import lax
from jax.experimental import pallas as pl
from jax.experimental.pallas import tpu as pltpu
from jax.sharding import Mesh
from jax.sharding import PartitionSpec as P

EXPERT_SLOTS = 4
SUBLANES = 8
LANES = 128
SPLIT = SUBLANES // EXPERT_SLOTS
eps = 1e-06
BF = jnp.bfloat16
F32 = jnp.float32
HIGHEST = lax.Precision.HIGHEST
VMEM = pl.BlockSpec(memory_space=pltpu.VMEM)
SMEM = pl.BlockSpec(memory_space=pltpu.SMEM)
HBM = pl.BlockSpec(memory_space=pltpu.HBM)
MIB = 1 << 20


def dot(a, b, precision=None):
    return jnp.dot(a, b, precision=precision, preferred_element_type=F32)


def iota(shape, axis):
    return lax.broadcasted_iota(jnp.int32, shape, axis)


def shift(x, axis, by):
    n = lax.axis_size(axis)
    return lax.ppermute(x, axis, [(i, (i + by) % n) for i in range(n)])


def stay(*arrays):
    return [pltpu.with_memory_space_constraint(a, pltpu.HBM) for a in arrays]


def early_kernel(his, los, partial_ref, hidden_ref, ids_hbm, prob_hbm, *refs):
    own_ref, held_ref, pick_ref, comb_ref, ids_ref, prob_ref, small, large = refs
    cols = hidden_ref.shape[1]
    l = lax.axis_index("lo")
    first = [
        pltpu.make_async_copy(ids_hbm, ids_ref, small.at[0]),
        pltpu.make_async_copy(prob_hbm, prob_ref, small.at[1]),
    ]
    rest = [pltpu.make_async_copy(hidden_ref, held_ref, large.at[his])]
    for x in range(his):
        at = pl.multiple_of((x * los + l) * cols, LANES)
        rest.append(
            pltpu.make_async_copy(
                partial_ref.at[0, :, pl.ds(at, cols)], own_ref.at[x], large.at[x]
            )
        )
    for copy in first + rest:
        copy.start()
    for copy in first:
        copy.wait()
    names, tokens = ids_ref.shape
    rows, wide = pick_ref.shape[1], comb_ref.shape[1]
    experts = rows // SUBLANES
    ids, prob = ids_ref[...], prob_ref[...].astype(F32)
    expert = iota((experts, tokens), 0)
    match = jnp.zeros((experts, tokens), F32)
    weight = jnp.zeros((experts, tokens), F32)
    for k in range(names):
        same = ids[k : k + 1] == expert
        match = match + jnp.where(same, 1.0, 0.0)
        weight = weight + jnp.where(same, prob[k : k + 1], 0.0)
    earlier = jnp.where(iota((tokens, tokens), 0) < iota((tokens, tokens), 1), 1.0, 0.0)
    slot = jnp.where(match > 0.0, dot(match, earlier, HIGHEST), -1.0)

    def spread(x, count, per):
        owner = jnp.where(iota((count, experts), 0) // per == iota((count, experts), 1), 1.0, 0.0)
        return dot(owner, x, HIGHEST)

    at = iota((rows, tokens), 0)
    slots = spread(slot, rows, SUBLANES)
    for s in range(SPLIT):
        here = (slots == (at % EXPERT_SLOTS).astype(F32)) & (at // EXPERT_SLOTS % SPLIT == s)
        pick_ref[s] = jnp.where(here, 1.0, 0.0).astype(BF)
    at = iota((wide, tokens), 0)
    per = his * EXPERT_SLOTS
    slots, weights = spread(slot, wide, per), spread(weight, wide, per)
    here = slots == (at % EXPERT_SLOTS).astype(F32)
    comb_ref[...] = jnp.where(here, weights, 0.0).T.astype(BF)
    for copy in rest:
        copy.wait()


def choose_kernel(los, pick_ref, own_ref, *refs):
    others, sel_ref, res_ref = refs[: los - 1], refs[los - 1], refs[los]
    his, _, cols = own_ref.shape
    width = cols // SPLIT
    h, l = lax.axis_index("hi"), lax.axis_index("lo")
    for k in range(1, his):
        hh = lax.rem(h + k, his)
        pair = own_ref[hh].astype(F32)
        at = pl.multiple_of((hh * los + l) * cols, LANES)
        for other in others:
            pair = pair + other[:, pl.ds(at, cols)].astype(F32)
        pair = pair.astype(BF)
        res_ref[k - 1] = pair
        chosen = dot(pick_ref[0], pair[:, :width])
        for s in range(1, SPLIT):
            chosen = chosen + dot(pick_ref[s], pair[:, s * width : (s + 1) * width])
        sel_ref[k - 1] = chosen.astype(BF)


def load_kernel(los, *refs):
    hbms, (hidden_ref, pick_ref, own_ref) = refs[:4], refs[4:7]
    others, (mine_ref, sel_ref), sems = refs[7 : 6 + los], refs[10 + los : 12 + los], refs[-1]
    copies = [
        pltpu.make_async_copy(hbm, vmem, sems.at[i])
        for i, (hbm, vmem) in enumerate(zip(hbms, refs[6 + los : 10 + los]))
    ]
    for copy in copies:
        copy.start()
    cols = hidden_ref.shape[1]
    width = cols // SPLIT
    h, l = lax.axis_index("hi"), lax.axis_index("lo")
    mine = hidden_ref[...].astype(F32) + own_ref[h].astype(F32)
    at = pl.multiple_of((h * los + l) * cols, LANES)
    for other in others:
        mine = mine + other[:, pl.ds(at, cols)].astype(F32)
    mine_ref[...] = mine
    chosen = dot(pick_ref[0].astype(F32), mine[:, :width], HIGHEST)
    for s in range(1, SPLIT):
        chosen = chosen + dot(
            pick_ref[s].astype(F32), mine[:, s * width : (s + 1) * width], HIGHEST
        )
    sel_ref[...] = chosen
    for copy in copies:
        copy.wait()


def dispatch_kernel(n, sel_ref, *refs):
    gots, out_ref = refs[:n], refs[n]
    experts, his, subs, width = out_ref.shape
    chosen = sel_ref[...]
    for got in gots:
        chosen = chosen + got[...].astype(F32)
    chosen = chosen.astype(BF).reshape(experts, subs, width)
    for x in range(his):
        out_ref[:, x] = chosen


def regroup(even, odd):
    top = iota(even.shape, 0) < EXPERT_SLOTS
    return (
        jnp.where(top, even, pltpu.roll(odd, EXPERT_SLOTS, 0)),
        jnp.where(top, pltpu.roll(even, EXPERT_SLOTS, 0), odd),
    )


def gather_rows(ref, x, experts):
    his = ref.shape[0] // experts
    low, high = [], []
    for p in range(0, experts, SPLIT):
        even, odd = ref[p * his + x].astype(F32), ref[(p + 1) * his + x].astype(F32)
        first, second = regroup(even, odd)
        low.append(first)
        high.append(second)
    return jnp.concatenate(
        [jnp.concatenate(low, axis=0), jnp.concatenate(high, axis=0)], axis=1
    )


def products(los, helds, gain_ref, wg_ref, wu_ref, gate, up, square, top):
    l, experts = lax.axis_index("lo"), lax.axis_size("dp")
    for k, held in helds:
        his = held.shape[0] // experts
        width = held.shape[2]
        cols = SPLIT * width
        c = lax.rem(l - k + los, los)
        for x in range(his):
            value = gather_rows(held, x, experts)
            at = pl.multiple_of((x * los + c) * cols, LANES)
            square = square + jnp.sum(value * value, axis=1, keepdims=True)
            value = value * gain_ref[:, pl.ds(at, cols)]
            top = jnp.maximum(top, jnp.max(jnp.abs(value), axis=1, keepdims=True))
            value = value.astype(BF)
            for n in range(0, cols, width):
                part, here = value[:, n : n + width], pl.ds(at + n, width)
                gate = gate + dot(part, wg_ref[0, here, :])
                up = up + dot(part, wu_ref[0, here, :])
    return gate, up, square, top


def first_kernel(los, gain_ref, wg_ref, wu_ref, held_ref, *refs):
    gate_ref, up_ref, square_ref, top_ref = refs
    slots = gate_ref.shape[0]
    zero, none = jnp.zeros(gate_ref.shape, F32), jnp.zeros((slots, 1), F32)
    gate, up, square, top = products(
        los, [(0, held_ref)], gain_ref, wg_ref, wu_ref, zero, zero, none, none
    )
    gate_ref[...] = gate
    up_ref[...] = up
    square_ref[...] = jnp.broadcast_to(square, square_ref.shape)
    top_ref[...] = jnp.broadcast_to(top, top_ref.shape)


def down(act, wd_ref, his, los, c):
    cols = wd_ref.shape[2] // (his * los)
    for x in range(his):
        at = pl.multiple_of((x * los + c) * cols, LANES)
        yield slice(x * cols, (x + 1) * cols), dot(act, wd_ref[0, :, pl.ds(at, cols)])


def second_kernel(his, los, gain_ref, wg_ref, wu_ref, wd_ref, *refs):
    gate_ref, up_ref, square_ref, top_ref = refs[:4]
    helds = refs[4 : 3 + los]
    send_ref, act_ref, peak_ref, out_ref = refs[3 + los :]
    gate, up, square, top = products(
        los,
        list(enumerate(helds, 1)),
        gain_ref,
        wg_ref,
        wu_ref,
        gate_ref[...],
        up_ref[...],
        square_ref[:, :1],
        top_ref[:, :1],
    )
    scale = lax.rsqrt(square / wg_ref.shape[1] + eps)
    out_ref[...] = jnp.full(out_ref.shape, jnp.max(top * scale), F32)
    gate, up = gate * scale, up * scale
    act = (gate / (1.0 + jnp.exp(-gate)) * up).astype(BF)
    act_ref[...] = act
    peak = jnp.max(jnp.abs(act.astype(F32)))
    peak_ref[...] = jnp.full(peak_ref.shape, peak, F32)
    for k in range(1, los):
        c = lax.rem(lax.axis_index("lo") + k, los)
        for cut, value in down(act, wd_ref, his, los, c):
            send_ref[k - 1, :, cut] = value.astype(BF)
        send_ref[k - 1, :, -LANES:] = jnp.full((act.shape[0], LANES), peak, F32).astype(BF)


def third_kernel(his, los, act_ref, wd_ref, keep_ref):
    for cut, value in down(act_ref[...], wd_ref, his, los, lax.axis_index("lo")):
        keep_ref[:, cut] = value


def pair_kernel(his, n, keep_ref, peak_ref, *refs):
    gots, out_ref = refs[:n], refs[n]
    experts, cols = out_ref.shape[0] // his, out_ref.shape[2] - LANES
    peak = peak_ref[:EXPERT_SLOTS]
    for got in gots:
        peak = jnp.maximum(peak, got[:EXPERT_SLOTS, -LANES:].astype(F32))
    for x in range(his):
        total = keep_ref[:, x * cols : (x + 1) * cols]
        for got in gots:
            total = total + got[:, x * cols : (x + 1) * cols].astype(F32)
        for e in range(experts):
            rows = total[e * EXPERT_SLOTS : (e + 1) * EXPERT_SLOTS]
            out_ref[e * his + x, :, :cols] = rows.astype(BF)
            out_ref[e * his + x, :, cols:] = peak.astype(BF)


def hold_kernel(his, back_ref, out_ref):
    peak = back_ref[pl.ds(lax.axis_index("dp") * his, his), :, -LANES:].astype(F32)
    out_ref[...] = jnp.max(peak, axis=0)


def combine_kernel(his, mine_ref, comb_ref, back_ref, top_ref, tile_ref, *refs):
    rests, (out_ref, input_ref, hidden_ref) = refs[: his - 1], refs[-3:]
    input_ref[0] = jnp.max(top_ref[...].astype(BF).astype(F32))
    hidden_ref[0] = jnp.max(tile_ref[...])
    blocks, slots, cols = back_ref.shape
    cols = cols - LANES
    back = back_ref[:, :, :cols].reshape(blocks * slots, cols)
    res = mine_ref[...]
    for rest in rests:
        res = res + rest[...].astype(F32)
    out_ref[...] = (res + dot(comb_ref[...], back)).astype(BF)


def call(kernel, mib, ins, outs, scratch=(), flops=0, moved=0):
    places = [SMEM if isinstance(o, jax.ShapeDtypeStruct) else VMEM for o in outs]
    return pl.pallas_call(
        kernel,
        out_shape=outs,
        in_specs=[HBM if at == "hbm" else VMEM for at, _ in ins],
        out_specs=places,
        scratch_shapes=scratch,
        compiler_params=pltpu.CompilerParams(vmem_limit_bytes=mib * MIB),
        cost_estimate=pl.CostEstimate(flops=flops, bytes_accessed=moved, transcendentals=0),
    )(*[stay(x)[0] if at == "hbm" else x for at, x in ins])


def near(*arrays):
    return [("vmem", a) for a in arrays]


def far(*arrays):
    return [("hbm", a) for a in arrays]


def on_device(attn_partial, hidden_in, norm_gain, expert_ids, route_prob, w_gate, w_up, w_down):
    experts, his, los = lax.axis_size("dp"), lax.axis_size("hi"), lax.axis_size("lo")
    tokens, cols = hidden_in.shape
    _, units = w_gate.shape[1:]
    width, blocks = cols // SPLIT, experts * his
    slots, rows = experts * EXPERT_SLOTS, experts * SUBLANES
    gain = norm_gain.reshape(1, -1)

    others = [shift(attn_partial[0], "lo", k) for k in range(1, los)]
    own, hidden, pick, comb = call(
        lambda *refs: early_kernel(his, los, *refs),
        4,
        far(attn_partial, hidden_in, expert_ids.T, route_prob.T),
        [
            pltpu.VMEM((his, tokens, cols), BF),
            pltpu.VMEM((tokens, cols), BF),
            pltpu.VMEM((SPLIT, rows, tokens), BF),
            pltpu.VMEM((tokens, blocks * EXPERT_SLOTS), BF),
        ],
        [
            pltpu.VMEM(expert_ids.shape[::-1], expert_ids.dtype),
            pltpu.VMEM(route_prob.shape[::-1], route_prob.dtype),
            pltpu.SemaphoreType.DMA((2,)),
            pltpu.SemaphoreType.DMA((his + 1,)),
        ],
        moved=MIB,
    )
    sels, rests = call(
        lambda *refs: choose_kernel(los, *refs),
        4,
        near(pick, own, *others),
        [
            pltpu.VMEM((his - 1, rows, width), BF),
            pltpu.VMEM((his - 1, tokens, cols), BF),
        ],
    )
    sels = [shift(sels[k - 1], "hi", k) for k in range(1, his)]
    gain, wg, wu, wd, mine, sel = call(
        lambda *refs: load_kernel(los, *refs),
        4,
        far(gain, w_gate, w_up, w_down) + near(hidden, pick, own, *others),
        [
            pltpu.VMEM(gain.shape, F32),
            pltpu.VMEM(w_gate.shape, BF),
            pltpu.VMEM(w_up.shape, BF),
            pltpu.VMEM(w_down.shape, BF),
            pltpu.VMEM((tokens, cols), F32),
            pltpu.VMEM((rows, width), F32),
        ],
        [pltpu.SemaphoreType.DMA((4,))],
        moved=12 * MIB,
    )
    (outgoing,) = call(
        lambda *refs: dispatch_kernel(his - 1, *refs),
        4,
        near(sel, *sels),
        [pltpu.VMEM((experts, his, SUBLANES, width), BF)],
    )
    incoming = lax.all_to_all(
        outgoing.reshape(blocks, SUBLANES, width), ("dp", "hi"), 0, 0, tiled=True
    )
    helds = [shift(incoming, "lo", k) for k in range(1, los)]
    rests = [shift(rests[k - 1], "hi", k) for k in range(1, his)]
    sums = call(
        lambda *refs: first_kernel(los, *refs),
        8,
        near(gain, wg, wu, incoming),
        [
            pltpu.VMEM((slots, units), F32),
            pltpu.VMEM((slots, units), F32),
            pltpu.VMEM((slots, LANES), F32),
            pltpu.VMEM((slots, LANES), F32),
        ],
        moved=4 * MIB,
    )
    sends, act, peak, top = call(
        lambda *refs: second_kernel(his, los, *refs),
        8,
        near(gain, wg, wu, wd, *sums, *helds),
        [
            pltpu.VMEM((los - 1, slots, his * cols + LANES), BF),
            pltpu.VMEM((slots, units), BF),
            pltpu.VMEM((SUBLANES, LANES), F32),
            pltpu.VMEM((SUBLANES, LANES), F32),
        ],
    )
    sends = [shift(sends[k - 1], "lo", k) for k in range(1, los)]
    (keep,) = call(
        lambda *refs: third_kernel(his, los, *refs),
        8,
        near(act, wd),
        [pltpu.VMEM((slots, his * cols), F32)],
        moved=2 * MIB,
    )
    (back,) = call(
        lambda *refs: pair_kernel(his, los - 1, *refs),
        4,
        near(keep, peak, *sends),
        [pltpu.VMEM((blocks, EXPERT_SLOTS, cols + LANES), BF)],
    )
    back = lax.all_to_all(back, ("dp", "hi"), 0, 0, tiled=True)
    (tile,) = call(
        lambda *refs: hold_kernel(his, *refs),
        1,
        near(back),
        [pltpu.VMEM((EXPERT_SLOTS, LANES), F32)],
    )
    layer_out, input_top, hidden_top = pl.pallas_call(
        lambda *refs: combine_kernel(his, *refs),
        out_shape=[
            jax.ShapeDtypeStruct((tokens, cols), BF),
            jax.ShapeDtypeStruct((1,), F32),
            jax.ShapeDtypeStruct((1,), F32),
        ],
        in_specs=[VMEM] * (4 + his),
        out_specs=[VMEM, SMEM, SMEM],
        compiler_params=pltpu.CompilerParams(vmem_limit_bytes=4 * MIB),
        name="combine",
    )(mine, comb, back, top, tile, *rests)
    return layer_out, input_top, hidden_top


def solution(mesh):
    tp = mesh.shape["tp"]
    lo = 2 if tp % 2 == 0 else 1
    split = Mesh(mesh.devices.reshape(mesh.shape["dp"], tp // lo, lo), ("dp", "hi", "lo"))
    tps = ("hi", "lo")
    placed = (
        P(tps, "dp", None),
        P("dp", tps),
        P(),
        P("dp", None),
        P("dp", None),
        P("dp", None, tps),
        P("dp", None, tps),
        P("dp", tps, None),
    )

    return jax.shard_map(
        on_device,
        mesh=split,
        in_specs=placed,
        out_specs=(P("dp", tps), P("dp"), P("dp")),
        check_vma=False,
    )
```

```python
import jax
import jax.numpy as jnp
from jax import lax
from jax.experimental import pallas as pl
from jax.experimental.pallas import tpu as pltpu
from jax.sharding import Mesh
from jax.sharding import PartitionSpec as P

EXPERT_SLOTS = 4
SUBLANES = 8
LANES = 128
SPLIT = SUBLANES // EXPERT_SLOTS
eps = 1e-06
BF = jnp.bfloat16
F32 = jnp.float32
HIGHEST = lax.Precision.HIGHEST
VMEM = pl.BlockSpec(memory_space=pltpu.VMEM)
SMEM = pl.BlockSpec(memory_space=pltpu.SMEM)
HBM = pl.BlockSpec(memory_space=pltpu.HBM)
MIB = 1 << 20


def dot(a, b, precision=None):
    return jnp.dot(a, b, precision=precision, preferred_element_type=F32)


def iota(shape, axis):
    return lax.broadcasted_iota(jnp.int32, shape, axis)


def shift(x, axis, by):
    n = lax.axis_size(axis)
    return lax.ppermute(x, axis, [(i, (i + by) % n) for i in range(n)])


def stay(*arrays):
    return [pltpu.with_memory_space_constraint(a, pltpu.HBM) for a in arrays]


def early_kernel(his, los, partial_ref, hidden_ref, ids_hbm, prob_hbm, up_hbm, *refs):
    own_ref, held_ref, pick_ref, comb_ref, up_ref, ids_ref, prob_ref, small, large = refs
    cols = hidden_ref.shape[1]
    l = lax.axis_index("lo")
    first = [
        pltpu.make_async_copy(ids_hbm, ids_ref, small.at[0]),
        pltpu.make_async_copy(prob_hbm, prob_ref, small.at[1]),
    ]
    rest = [pltpu.make_async_copy(hidden_ref, held_ref, large.at[his])]
    for x in range(his):
        at = pl.multiple_of((x * los + l) * cols, LANES)
        rest.append(
            pltpu.make_async_copy(
                partial_ref.at[0, :, pl.ds(at, cols)], own_ref.at[x], large.at[x]
            )
        )
    part = up_hbm.at[:, pl.ds(0, up_ref.shape[1]), :]
    rest.append(pltpu.make_async_copy(part, up_ref, large.at[his + 1]))
    for copy in first + rest:
        copy.start()
    for copy in first:
        copy.wait()
    names, tokens = ids_ref.shape
    rows, wide = pick_ref.shape[1], comb_ref.shape[1]
    experts = rows // SUBLANES
    ids, prob = ids_ref[...], prob_ref[...].astype(F32)
    expert = iota((experts, tokens), 0)
    match = jnp.zeros((experts, tokens), F32)
    weight = jnp.zeros((experts, tokens), F32)
    for k in range(names):
        same = ids[k : k + 1] == expert
        match = match + jnp.where(same, 1.0, 0.0)
        weight = weight + jnp.where(same, prob[k : k + 1], 0.0)
    earlier = jnp.where(iota((tokens, tokens), 0) < iota((tokens, tokens), 1), 1.0, 0.0)
    slot = jnp.where(match > 0.0, dot(match, earlier, HIGHEST), -1.0)

    def spread(x, count, per):
        owner = jnp.where(iota((count, experts), 0) // per == iota((count, experts), 1), 1.0, 0.0)
        return dot(owner, x, HIGHEST)

    at = iota((rows, tokens), 0)
    slots = spread(slot, rows, SUBLANES)
    for s in range(SPLIT):
        here = (slots == (at % EXPERT_SLOTS).astype(F32)) & (at // EXPERT_SLOTS % SPLIT == s)
        pick_ref[s] = jnp.where(here, 1.0, 0.0).astype(BF)
    at = iota((wide, tokens), 0)
    per = his * EXPERT_SLOTS
    slots, weights = spread(slot, wide, per), spread(weight, wide, per)
    here = slots == (at % EXPERT_SLOTS).astype(F32)
    comb_ref[...] = jnp.where(here, weights, 0.0).T.astype(BF)
    for copy in rest:
        copy.wait()


def choose_kernel(los, pick_ref, own_ref, *refs):
    others, sel_ref, res_ref = refs[: los - 1], refs[los - 1], refs[los]
    his, _, cols = own_ref.shape
    width = cols // SPLIT
    h, l = lax.axis_index("hi"), lax.axis_index("lo")
    for k in range(1, his):
        hh = lax.rem(h + k, his)
        pair = own_ref[hh].astype(F32)
        at = pl.multiple_of((hh * los + l) * cols, LANES)
        for other in others:
            pair = pair + other[:, pl.ds(at, cols)].astype(F32)
        pair = pair.astype(BF)
        res_ref[k - 1] = pair
        chosen = dot(pick_ref[0], pair[:, :width])
        for s in range(1, SPLIT):
            chosen = chosen + dot(pick_ref[s], pair[:, s * width : (s + 1) * width])
        sel_ref[k - 1] = chosen.astype(BF)


def load_kernel(los, *refs):
    hbms, (hidden_ref, pick_ref, own_ref) = refs[:4], refs[4:7]
    others, (mine_ref, sel_ref), sems = refs[7 : 6 + los], refs[10 + los : 12 + los], refs[-1]
    copies = [
        pltpu.make_async_copy(
            hbm if i != 2 else hbm.at[:, pl.ds(hbm.shape[1] - vmem.shape[1], vmem.shape[1]), :],
            vmem,
            sems.at[i],
        )
        for i, (hbm, vmem) in enumerate(zip(hbms, refs[6 + los : 10 + los]))
    ]
    for copy in copies:
        copy.start()
    cols = hidden_ref.shape[1]
    width = cols // SPLIT
    h, l = lax.axis_index("hi"), lax.axis_index("lo")
    mine = hidden_ref[...].astype(F32) + own_ref[h].astype(F32)
    at = pl.multiple_of((h * los + l) * cols, LANES)
    for other in others:
        mine = mine + other[:, pl.ds(at, cols)].astype(F32)
    mine_ref[...] = mine
    chosen = dot(pick_ref[0].astype(F32), mine[:, :width], HIGHEST)
    for s in range(1, SPLIT):
        chosen = chosen + dot(
            pick_ref[s].astype(F32), mine[:, s * width : (s + 1) * width], HIGHEST
        )
    sel_ref[...] = chosen
    for copy in copies:
        copy.wait()


def dispatch_kernel(n, sel_ref, *refs):
    gots, out_ref = refs[:n], refs[n]
    experts, his, subs, width = out_ref.shape
    chosen = sel_ref[...]
    for got in gots:
        chosen = chosen + got[...].astype(F32)
    chosen = chosen.astype(BF).reshape(experts, subs, width)
    for x in range(his):
        out_ref[:, x] = chosen


def regroup(even, odd):
    top = iota(even.shape, 0) < EXPERT_SLOTS
    return (
        jnp.where(top, even, pltpu.roll(odd, EXPERT_SLOTS, 0)),
        jnp.where(top, pltpu.roll(even, EXPERT_SLOTS, 0), odd),
    )


def gather_rows(ref, x, experts):
    his = ref.shape[0] // experts
    low, high = [], []
    for p in range(0, experts, SPLIT):
        even, odd = ref[p * his + x].astype(F32), ref[(p + 1) * his + x].astype(F32)
        first, second = regroup(even, odd)
        low.append(first)
        high.append(second)
    return jnp.concatenate(
        [jnp.concatenate(low, axis=0), jnp.concatenate(high, axis=0)], axis=1
    )


def products(los, helds, gain_ref, wg_ref, wu_refs, gate, up, square, top):
    l, experts = lax.axis_index("lo"), lax.axis_size("dp")
    for k, held in helds:
        his = held.shape[0] // experts
        width = held.shape[2]
        cols = SPLIT * width
        c = lax.rem(l - k + los, los)
        for x in range(his):
            value = gather_rows(held, x, experts)
            at = pl.multiple_of((x * los + c) * cols, LANES)
            square = square + jnp.sum(value * value, axis=1, keepdims=True)
            value = value * gain_ref[:, pl.ds(at, cols)]
            top = jnp.maximum(top, jnp.max(jnp.abs(value), axis=1, keepdims=True))
            value = value.astype(BF)
            for n in range(0, cols, width):
                part, here = value[:, n : n + width], pl.ds(at + n, width)
                gate = gate + dot(part, wg_ref[0, here, :])
                wu_ref, base = (wu_refs[0], 0) if x == 0 else (wu_refs[1], los * cols)
                up = up + dot(part, wu_ref[0, pl.ds(at + n - base, width), :])
    return gate, up, square, top


def first_kernel(los, gain_ref, wg_ref, wu_first, wu_rest, held_ref, *refs):
    gate_ref, up_ref, square_ref, top_ref = refs
    slots = gate_ref.shape[0]
    zero, none = jnp.zeros(gate_ref.shape, F32), jnp.zeros((slots, 1), F32)
    gate, up, square, top = products(
        los, [(0, held_ref)], gain_ref, wg_ref, (wu_first, wu_rest), zero, zero, none, none
    )
    gate_ref[...] = gate
    up_ref[...] = up
    square_ref[...] = jnp.broadcast_to(square, square_ref.shape)
    top_ref[...] = jnp.broadcast_to(top, top_ref.shape)


def down(act, wd_ref, his, los, c):
    cols = wd_ref.shape[2] // (his * los)
    for x in range(his):
        at = pl.multiple_of((x * los + c) * cols, LANES)
        yield slice(x * cols, (x + 1) * cols), dot(act, wd_ref[0, :, pl.ds(at, cols)])


def second_kernel(his, los, gain_ref, wg_ref, wu_first, wu_rest, wd_ref, *refs):
    gate_ref, up_ref, square_ref, top_ref = refs[:4]
    helds = refs[4 : 3 + los]
    send_ref, act_ref, peak_ref, out_ref = refs[3 + los :]
    gate, up, square, top = products(
        los,
        list(enumerate(helds, 1)),
        gain_ref,
        wg_ref,
        (wu_first, wu_rest),
        gate_ref[...],
        up_ref[...],
        square_ref[:, :1],
        top_ref[:, :1],
    )
    scale = lax.rsqrt(square / wg_ref.shape[1] + eps)
    out_ref[...] = jnp.full(out_ref.shape, jnp.max(top * scale), F32)
    gate, up = gate * scale, up * scale
    act = (gate / (1.0 + jnp.exp(-gate)) * up).astype(BF)
    act_ref[...] = act
    peak = jnp.max(jnp.abs(act.astype(F32)))
    peak_ref[...] = jnp.full(peak_ref.shape, peak, F32)
    for k in range(1, los):
        c = lax.rem(lax.axis_index("lo") + k, los)
        for cut, value in down(act, wd_ref, his, los, c):
            send_ref[k - 1, :, cut] = value.astype(BF)
        send_ref[k - 1, :, -LANES:] = jnp.full((act.shape[0], LANES), peak, F32).astype(BF)


def third_kernel(his, los, act_ref, wd_ref, keep_ref):
    for cut, value in down(act_ref[...], wd_ref, his, los, lax.axis_index("lo")):
        keep_ref[:, cut] = value


def pair_kernel(his, n, keep_ref, peak_ref, *refs):
    gots, out_ref = refs[:n], refs[n]
    experts, cols = out_ref.shape[0] // his, out_ref.shape[2] - LANES
    peak = peak_ref[:EXPERT_SLOTS]
    for got in gots:
        peak = jnp.maximum(peak, got[:EXPERT_SLOTS, -LANES:].astype(F32))
    for x in range(his):
        total = keep_ref[:, x * cols : (x + 1) * cols]
        for got in gots:
            total = total + got[:, x * cols : (x + 1) * cols].astype(F32)
        for e in range(experts):
            rows = total[e * EXPERT_SLOTS : (e + 1) * EXPERT_SLOTS]
            out_ref[e * his + x, :, :cols] = rows.astype(BF)
            out_ref[e * his + x, :, cols:] = peak.astype(BF)


def hold_kernel(his, back_ref, out_ref):
    peak = back_ref[pl.ds(lax.axis_index("dp") * his, his), :, -LANES:].astype(F32)
    out_ref[...] = jnp.max(peak, axis=0)


def combine_kernel(his, mine_ref, comb_ref, back_ref, top_ref, tile_ref, *refs):
    rests, (out_ref, input_ref, hidden_ref) = refs[: his - 1], refs[-3:]
    input_ref[0] = jnp.max(top_ref[...].astype(BF).astype(F32))
    hidden_ref[0] = jnp.max(tile_ref[...])
    blocks, slots, cols = back_ref.shape
    cols = cols - LANES
    back = back_ref[:, :, :cols].reshape(blocks * slots, cols)
    res = mine_ref[...]
    for rest in rests:
        res = res + rest[...].astype(F32)
    out_ref[...] = (res + dot(comb_ref[...], back)).astype(BF)


def call(kernel, mib, ins, outs, scratch=(), flops=0, moved=0):
    places = [SMEM if isinstance(o, jax.ShapeDtypeStruct) else VMEM for o in outs]
    return pl.pallas_call(
        kernel,
        out_shape=outs,
        in_specs=[HBM if at == "hbm" else VMEM for at, _ in ins],
        out_specs=places,
        scratch_shapes=scratch,
        compiler_params=pltpu.CompilerParams(vmem_limit_bytes=mib * MIB),
        cost_estimate=pl.CostEstimate(flops=flops, bytes_accessed=moved, transcendentals=0),
    )(*[stay(x)[0] if at == "hbm" else x for at, x in ins])


def near(*arrays):
    return [("vmem", a) for a in arrays]


def far(*arrays):
    return [("hbm", a) for a in arrays]


def on_device(attn_partial, hidden_in, norm_gain, expert_ids, route_prob, w_gate, w_up, w_down):
    experts, his, los = lax.axis_size("dp"), lax.axis_size("hi"), lax.axis_size("lo")
    tokens, cols = hidden_in.shape
    features, units = w_gate.shape[1:]
    width, blocks = cols // SPLIT, experts * his
    slots, rows = experts * EXPERT_SLOTS, experts * SUBLANES
    gain = norm_gain.reshape(1, -1)

    others = [shift(attn_partial[0], "lo", k) for k in range(1, los)]
    own, hidden, pick, comb, wu_first = call(
        lambda *refs: early_kernel(his, los, *refs),
        4,
        far(attn_partial, hidden_in, expert_ids.T, route_prob.T, w_up),
        [
            pltpu.VMEM((his, tokens, cols), BF),
            pltpu.VMEM((tokens, cols), BF),
            pltpu.VMEM((SPLIT, rows, tokens), BF),
            pltpu.VMEM((tokens, blocks * EXPERT_SLOTS), BF),
            pltpu.VMEM((1, features // his, units), BF),
        ],
        [
            pltpu.VMEM(expert_ids.shape[::-1], expert_ids.dtype),
            pltpu.VMEM(route_prob.shape[::-1], route_prob.dtype),
            pltpu.SemaphoreType.DMA((2,)),
            pltpu.SemaphoreType.DMA((his + 2,)),
        ],
        moved=MIB,
    )
    sels, rests = call(
        lambda *refs: choose_kernel(los, *refs),
        4,
        near(pick, own, *others),
        [
            pltpu.VMEM((his - 1, rows, width), BF),
            pltpu.VMEM((his - 1, tokens, cols), BF),
        ],
    )
    sels = [shift(sels[k - 1], "hi", k) for k in range(1, his)]
    gain, wg, wu_rest, wd, mine, sel = call(
        lambda *refs: load_kernel(los, *refs),
        4,
        far(gain, w_gate, w_up, w_down) + near(hidden, pick, own, *others),
        [
            pltpu.VMEM(gain.shape, F32),
            pltpu.VMEM(w_gate.shape, BF),
            pltpu.VMEM((1, features - features // his, units), BF),
            pltpu.VMEM(w_down.shape, BF),
            pltpu.VMEM((tokens, cols), F32),
            pltpu.VMEM((rows, width), F32),
        ],
        [pltpu.SemaphoreType.DMA((4,))],
        moved=12 * MIB,
    )
    (outgoing,) = call(
        lambda *refs: dispatch_kernel(his - 1, *refs),
        4,
        near(sel, *sels),
        [pltpu.VMEM((experts, his, SUBLANES, width), BF)],
    )
    incoming = lax.all_to_all(
        outgoing.reshape(blocks, SUBLANES, width), ("dp", "hi"), 0, 0, tiled=True
    )
    helds = [shift(incoming, "lo", k) for k in range(1, los)]
    rests = [shift(rests[k - 1], "hi", k) for k in range(1, his)]
    sums = call(
        lambda *refs: first_kernel(los, *refs),
        8,
        near(gain, wg, wu_first, wu_rest, incoming),
        [
            pltpu.VMEM((slots, units), F32),
            pltpu.VMEM((slots, units), F32),
            pltpu.VMEM((slots, LANES), F32),
            pltpu.VMEM((slots, LANES), F32),
        ],
        moved=4 * MIB,
    )
    sends, act, peak, top = call(
        lambda *refs: second_kernel(his, los, *refs),
        8,
        near(gain, wg, wu_first, wu_rest, wd, *sums, *helds),
        [
            pltpu.VMEM((los - 1, slots, his * cols + LANES), BF),
            pltpu.VMEM((slots, units), BF),
            pltpu.VMEM((SUBLANES, LANES), F32),
            pltpu.VMEM((SUBLANES, LANES), F32),
        ],
    )
    sends = [shift(sends[k - 1], "lo", k) for k in range(1, los)]
    (keep,) = call(
        lambda *refs: third_kernel(his, los, *refs),
        8,
        near(act, wd),
        [pltpu.VMEM((slots, his * cols), F32)],
        moved=2 * MIB,
    )
    (back,) = call(
        lambda *refs: pair_kernel(his, los - 1, *refs),
        4,
        near(keep, peak, *sends),
        [pltpu.VMEM((blocks, EXPERT_SLOTS, cols + LANES), BF)],
    )
    back = lax.all_to_all(back, ("dp", "hi"), 0, 0, tiled=True)
    (tile,) = call(
        lambda *refs: hold_kernel(his, *refs),
        1,
        near(back),
        [pltpu.VMEM((EXPERT_SLOTS, LANES), F32)],
    )
    layer_out, input_top, hidden_top = pl.pallas_call(
        lambda *refs: combine_kernel(his, *refs),
        out_shape=[
            jax.ShapeDtypeStruct((tokens, cols), BF),
            jax.ShapeDtypeStruct((1,), F32),
            jax.ShapeDtypeStruct((1,), F32),
        ],
        in_specs=[VMEM] * (4 + his),
        out_specs=[VMEM, SMEM, SMEM],
        compiler_params=pltpu.CompilerParams(vmem_limit_bytes=4 * MIB),
        name="combine",
    )(mine, comb, back, top, tile, *rests)
    return layer_out, input_top, hidden_top


def solution(mesh):
    tp = mesh.shape["tp"]
    lo = 2 if tp % 2 == 0 else 1
    split = Mesh(mesh.devices.reshape(mesh.shape["dp"], tp // lo, lo), ("dp", "hi", "lo"))
    tps = ("hi", "lo")
    placed = (
        P(tps, "dp", None),
        P("dp", tps),
        P(),
        P("dp", None),
        P("dp", None),
        P("dp", None, tps),
        P("dp", None, tps),
        P("dp", tps, None),
    )

    return jax.shard_map(
        on_device,
        mesh=split,
        in_specs=placed,
        out_specs=(P("dp", tps), P("dp"), P("dp")),
        check_vma=False,
    )
```

```python
import jax
import jax.numpy as jnp
from jax import lax
from jax.experimental import pallas as pl
from jax.experimental.pallas import tpu as pltpu
from jax.sharding import Mesh
from jax.sharding import PartitionSpec as P

EXPERT_SLOTS = 4
SUBLANES = 8
LANES = 128
SPLIT = SUBLANES // EXPERT_SLOTS
eps = 1e-06
BF = jnp.bfloat16
F32 = jnp.float32
HIGHEST = lax.Precision.HIGHEST
VMEM = pl.BlockSpec(memory_space=pltpu.VMEM)
SMEM = pl.BlockSpec(memory_space=pltpu.SMEM)
HBM = pl.BlockSpec(memory_space=pltpu.HBM)
MIB = 1 << 20


def dot(a, b, precision=None):
    return jnp.dot(a, b, precision=precision, preferred_element_type=F32)


def iota(shape, axis):
    return lax.broadcasted_iota(jnp.int32, shape, axis)


def shift(x, axis, by):
    n = lax.axis_size(axis)
    return lax.ppermute(x, axis, [(i, (i + by) % n) for i in range(n)])


def stay(*arrays):
    return [pltpu.with_memory_space_constraint(a, pltpu.HBM) for a in arrays]


def early_kernel(his, los, partial_ref, hidden_ref, ids_hbm, prob_hbm, up_hbm, *refs):
    own_ref, held_ref, pick_ref, comb_ref, up_ref, ids_ref, prob_ref, small, large = refs
    cols = hidden_ref.shape[1]
    l = lax.axis_index("lo")
    first = [
        pltpu.make_async_copy(ids_hbm, ids_ref, small.at[0]),
        pltpu.make_async_copy(prob_hbm, prob_ref, small.at[1]),
    ]
    rest = [pltpu.make_async_copy(hidden_ref, held_ref, large.at[his])]
    for x in range(his):
        at = pl.multiple_of((x * los + l) * cols, LANES)
        rest.append(
            pltpu.make_async_copy(
                partial_ref.at[0, :, pl.ds(at, cols)], own_ref.at[x], large.at[x]
            )
        )
    part = up_hbm.at[:, pl.ds(0, up_ref.shape[1]), :]
    rest.append(pltpu.make_async_copy(part, up_ref, large.at[his + 1]))
    for copy in first + rest:
        copy.start()
    for copy in first:
        copy.wait()
    names, tokens = ids_ref.shape
    rows, wide = pick_ref.shape[1], comb_ref.shape[1]
    experts = rows // SUBLANES
    ids, prob = ids_ref[...], prob_ref[...].astype(F32)
    expert = iota((experts, tokens), 0)
    match = jnp.zeros((experts, tokens), F32)
    weight = jnp.zeros((experts, tokens), F32)
    for k in range(names):
        same = ids[k : k + 1] == expert
        match = match + jnp.where(same, 1.0, 0.0)
        weight = weight + jnp.where(same, prob[k : k + 1], 0.0)
    earlier = jnp.where(iota((tokens, tokens), 0) < iota((tokens, tokens), 1), 1.0, 0.0)
    slot = jnp.where(match > 0.0, dot(match, earlier, HIGHEST), -1.0)

    def spread(x, count, per):
        owner = jnp.where(iota((count, experts), 0) // per == iota((count, experts), 1), 1.0, 0.0)
        return dot(owner, x, HIGHEST)

    at = iota((rows, tokens), 0)
    slots = spread(slot, rows, SUBLANES)
    for s in range(SPLIT):
        here = (slots == (at % EXPERT_SLOTS).astype(F32)) & (at // EXPERT_SLOTS % SPLIT == s)
        pick_ref[s] = jnp.where(here, 1.0, 0.0).astype(BF)
    at = iota((wide, tokens), 0)
    per = his * EXPERT_SLOTS
    slots, weights = spread(slot, wide, per), spread(weight, wide, per)
    here = slots == (at % EXPERT_SLOTS).astype(F32)
    comb_ref[...] = jnp.where(here, weights, 0.0).T.astype(BF)
    for copy in rest:
        copy.wait()


def choose_kernel(los, pick_ref, own_ref, *refs):
    others, sel_ref = refs[: los - 1], refs[los - 1]
    his, _, cols = own_ref.shape
    width = cols // SPLIT
    h, l = lax.axis_index("hi"), lax.axis_index("lo")
    for k in range(1, his):
        hh = lax.rem(h + k, his)
        pair = own_ref[hh].astype(F32)
        at = pl.multiple_of((hh * los + l) * cols, LANES)
        for other in others:
            pair = pair + other[:, pl.ds(at, cols)].astype(F32)
        pair = pair.astype(BF)
        chosen = dot(pick_ref[0], pair[:, :width])
        for s in range(1, SPLIT):
            chosen = chosen + dot(pick_ref[s], pair[:, s * width : (s + 1) * width])
        sel_ref[k - 1] = chosen.astype(BF)


def load_kernel(los, *refs):
    hbms, (hidden_ref, pick_ref, own_ref) = refs[:4], refs[4:7]
    others, (mine_ref, sel_ref, res_ref), sems = refs[7 : 6 + los], refs[10 + los : -1], refs[-1]
    copies = [
        pltpu.make_async_copy(
            hbm if i != 2 else hbm.at[:, pl.ds(hbm.shape[1] - vmem.shape[1], vmem.shape[1]), :],
            vmem,
            sems.at[i],
        )
        for i, (hbm, vmem) in enumerate(zip(hbms, refs[6 + los : 10 + los]))
    ]
    for copy in copies:
        copy.start()
    cols = hidden_ref.shape[1]
    width = cols // SPLIT
    h, l = lax.axis_index("hi"), lax.axis_index("lo")
    mine = hidden_ref[...].astype(F32) + own_ref[h].astype(F32)
    at = pl.multiple_of((h * los + l) * cols, LANES)
    for other in others:
        mine = mine + other[:, pl.ds(at, cols)].astype(F32)
    mine_ref[...] = mine
    his = own_ref.shape[0]
    for k in range(1, his):
        hh = lax.rem(h + k, his)
        pair = own_ref[hh].astype(F32)
        at = pl.multiple_of((hh * los + l) * cols, LANES)
        for other in others:
            pair = pair + other[:, pl.ds(at, cols)].astype(F32)
        res_ref[k - 1] = pair.astype(BF)
    chosen = dot(pick_ref[0].astype(F32), mine[:, :width], HIGHEST)
    for s in range(1, SPLIT):
        chosen = chosen + dot(
            pick_ref[s].astype(F32), mine[:, s * width : (s + 1) * width], HIGHEST
        )
    sel_ref[...] = chosen
    for copy in copies:
        copy.wait()


def dispatch_kernel(n, sel_ref, *refs):
    gots, out_ref = refs[:n], refs[n]
    experts, his, subs, width = out_ref.shape
    chosen = sel_ref[...]
    for got in gots:
        chosen = chosen + got[...].astype(F32)
    chosen = chosen.astype(BF).reshape(experts, subs, width)
    for x in range(his):
        out_ref[:, x] = chosen


def regroup(even, odd):
    top = iota(even.shape, 0) < EXPERT_SLOTS
    return (
        jnp.where(top, even, pltpu.roll(odd, EXPERT_SLOTS, 0)),
        jnp.where(top, pltpu.roll(even, EXPERT_SLOTS, 0), odd),
    )


def gather_rows(ref, x, experts):
    his = ref.shape[0] // experts
    low, high = [], []
    for p in range(0, experts, SPLIT):
        even, odd = ref[p * his + x].astype(F32), ref[(p + 1) * his + x].astype(F32)
        first, second = regroup(even, odd)
        low.append(first)
        high.append(second)
    return jnp.concatenate(
        [jnp.concatenate(low, axis=0), jnp.concatenate(high, axis=0)], axis=1
    )


def products(los, helds, gain_ref, wg_ref, wu_refs, gate, up, square, top):
    l, experts = lax.axis_index("lo"), lax.axis_size("dp")
    for k, held in helds:
        his = held.shape[0] // experts
        width = held.shape[2]
        cols = SPLIT * width
        c = lax.rem(l - k + los, los)
        for x in range(his):
            value = gather_rows(held, x, experts)
            at = pl.multiple_of((x * los + c) * cols, LANES)
            square = square + jnp.sum(value * value, axis=1, keepdims=True)
            value = value * gain_ref[:, pl.ds(at, cols)]
            top = jnp.maximum(top, jnp.max(jnp.abs(value), axis=1, keepdims=True))
            value = value.astype(BF)
            for n in range(0, cols, width):
                part, here = value[:, n : n + width], pl.ds(at + n, width)
                gate = gate + dot(part, wg_ref[0, here, :])
                wu_ref, base = (wu_refs[0], 0) if x == 0 else (wu_refs[1], los * cols)
                up = up + dot(part, wu_ref[0, pl.ds(at + n - base, width), :])
    return gate, up, square, top


def first_kernel(los, gain_ref, wg_ref, wu_first, wu_rest, held_ref, *refs):
    gate_ref, up_ref, square_ref, top_ref = refs
    slots = gate_ref.shape[0]
    zero, none = jnp.zeros(gate_ref.shape, F32), jnp.zeros((slots, 1), F32)
    gate, up, square, top = products(
        los, [(0, held_ref)], gain_ref, wg_ref, (wu_first, wu_rest), zero, zero, none, none
    )
    gate_ref[...] = gate
    up_ref[...] = up
    square_ref[...] = jnp.broadcast_to(square, square_ref.shape)
    top_ref[...] = jnp.broadcast_to(top, top_ref.shape)


def down(act, wd_ref, his, los, c):
    cols = wd_ref.shape[2] // (his * los)
    for x in range(his):
        at = pl.multiple_of((x * los + c) * cols, LANES)
        yield slice(x * cols, (x + 1) * cols), dot(act, wd_ref[0, :, pl.ds(at, cols)])


def second_kernel(his, los, gain_ref, wg_ref, wu_first, wu_rest, wd_ref, *refs):
    gate_ref, up_ref, square_ref, top_ref = refs[:4]
    helds = refs[4 : 3 + los]
    send_ref, act_ref, peak_ref, out_ref = refs[3 + los :]
    gate, up, square, top = products(
        los,
        list(enumerate(helds, 1)),
        gain_ref,
        wg_ref,
        (wu_first, wu_rest),
        gate_ref[...],
        up_ref[...],
        square_ref[:, :1],
        top_ref[:, :1],
    )
    scale = lax.rsqrt(square / wg_ref.shape[1] + eps)
    out_ref[...] = jnp.full(out_ref.shape, jnp.max(top * scale), F32)
    gate, up = gate * scale, up * scale
    act = (gate / (1.0 + jnp.exp(-gate)) * up).astype(BF)
    act_ref[...] = act
    peak = jnp.max(jnp.abs(act.astype(F32)))
    peak_ref[...] = jnp.full(peak_ref.shape, peak, F32)
    for k in range(1, los):
        c = lax.rem(lax.axis_index("lo") + k, los)
        for cut, value in down(act, wd_ref, his, los, c):
            send_ref[k - 1, :, cut] = value.astype(BF)
        send_ref[k - 1, :, -LANES:] = jnp.full((act.shape[0], LANES), peak, F32).astype(BF)


def third_kernel(his, los, act_ref, wd_ref, keep_ref):
    for cut, value in down(act_ref[...], wd_ref, his, los, lax.axis_index("lo")):
        keep_ref[:, cut] = value


def pair_kernel(his, n, keep_ref, peak_ref, *refs):
    gots, out_ref = refs[:n], refs[n]
    experts, cols = out_ref.shape[0] // his, out_ref.shape[2] - LANES
    peak = peak_ref[:EXPERT_SLOTS]
    for got in gots:
        peak = jnp.maximum(peak, got[:EXPERT_SLOTS, -LANES:].astype(F32))
    for x in range(his):
        total = keep_ref[:, x * cols : (x + 1) * cols]
        for got in gots:
            total = total + got[:, x * cols : (x + 1) * cols].astype(F32)
        for e in range(experts):
            rows = total[e * EXPERT_SLOTS : (e + 1) * EXPERT_SLOTS]
            out_ref[e * his + x, :, :cols] = rows.astype(BF)
            out_ref[e * his + x, :, cols:] = peak.astype(BF)


def hold_kernel(his, back_ref, out_ref):
    peak = back_ref[pl.ds(lax.axis_index("dp") * his, his), :, -LANES:].astype(F32)
    out_ref[...] = jnp.max(peak, axis=0)


def combine_kernel(his, mine_ref, comb_ref, back_ref, top_ref, tile_ref, *refs):
    rests, (out_ref, input_ref, hidden_ref) = refs[: his - 1], refs[-3:]
    input_ref[0] = jnp.max(top_ref[...].astype(BF).astype(F32))
    hidden_ref[0] = jnp.max(tile_ref[...])
    blocks, slots, cols = back_ref.shape
    cols = cols - LANES
    back = back_ref[:, :, :cols].reshape(blocks * slots, cols)
    res = mine_ref[...]
    for rest in rests:
        res = res + rest[...].astype(F32)
    out_ref[...] = (res + dot(comb_ref[...], back)).astype(BF)


def call(kernel, mib, ins, outs, scratch=(), flops=0, moved=0):
    places = [SMEM if isinstance(o, jax.ShapeDtypeStruct) else VMEM for o in outs]
    return pl.pallas_call(
        kernel,
        out_shape=outs,
        in_specs=[HBM if at == "hbm" else VMEM for at, _ in ins],
        out_specs=places,
        scratch_shapes=scratch,
        compiler_params=pltpu.CompilerParams(vmem_limit_bytes=mib * MIB),
        cost_estimate=pl.CostEstimate(flops=flops, bytes_accessed=moved, transcendentals=0),
    )(*[stay(x)[0] if at == "hbm" else x for at, x in ins])


def near(*arrays):
    return [("vmem", a) for a in arrays]


def far(*arrays):
    return [("hbm", a) for a in arrays]


def on_device(attn_partial, hidden_in, norm_gain, expert_ids, route_prob, w_gate, w_up, w_down):
    experts, his, los = lax.axis_size("dp"), lax.axis_size("hi"), lax.axis_size("lo")
    tokens, cols = hidden_in.shape
    features, units = w_gate.shape[1:]
    width, blocks = cols // SPLIT, experts * his
    slots, rows = experts * EXPERT_SLOTS, experts * SUBLANES
    gain = norm_gain.reshape(1, -1)

    others = [shift(attn_partial[0], "lo", k) for k in range(1, los)]
    own, hidden, pick, comb, wu_first = call(
        lambda *refs: early_kernel(his, los, *refs),
        4,
        far(attn_partial, hidden_in, expert_ids.T, route_prob.T, w_up),
        [
            pltpu.VMEM((his, tokens, cols), BF),
            pltpu.VMEM((tokens, cols), BF),
            pltpu.VMEM((SPLIT, rows, tokens), BF),
            pltpu.VMEM((tokens, blocks * EXPERT_SLOTS), BF),
            pltpu.VMEM((1, features // his, units), BF),
        ],
        [
            pltpu.VMEM(expert_ids.shape[::-1], expert_ids.dtype),
            pltpu.VMEM(route_prob.shape[::-1], route_prob.dtype),
            pltpu.SemaphoreType.DMA((2,)),
            pltpu.SemaphoreType.DMA((his + 2,)),
        ],
        moved=MIB,
    )
    (sels,) = call(
        lambda *refs: choose_kernel(los, *refs),
        4,
        near(pick, own, *others),
        [
            pltpu.VMEM((his - 1, rows, width), BF),
        ],
    )
    sels = [shift(sels[k - 1], "hi", k) for k in range(1, his)]
    gain, wg, wu_rest, wd, mine, sel, rests = call(
        lambda *refs: load_kernel(los, *refs),
        4,
        far(gain, w_gate, w_up, w_down) + near(hidden, pick, own, *others),
        [
            pltpu.VMEM(gain.shape, F32),
            pltpu.VMEM(w_gate.shape, BF),
            pltpu.VMEM((1, features - features // his, units), BF),
            pltpu.VMEM(w_down.shape, BF),
            pltpu.VMEM((tokens, cols), F32),
            pltpu.VMEM((rows, width), F32),
            pltpu.VMEM((his - 1, tokens, cols), BF),
        ],
        [pltpu.SemaphoreType.DMA((4,))],
        moved=12 * MIB,
    )
    (outgoing,) = call(
        lambda *refs: dispatch_kernel(his - 1, *refs),
        4,
        near(sel, *sels),
        [pltpu.VMEM((experts, his, SUBLANES, width), BF)],
    )
    incoming = lax.all_to_all(
        outgoing.reshape(blocks, SUBLANES, width), ("dp", "hi"), 0, 0, tiled=True
    )
    helds = [shift(incoming, "lo", k) for k in range(1, los)]
    rests = [shift(rests[k - 1], "hi", k) for k in range(1, his)]
    sums = call(
        lambda *refs: first_kernel(los, *refs),
        8,
        near(gain, wg, wu_first, wu_rest, incoming),
        [
            pltpu.VMEM((slots, units), F32),
            pltpu.VMEM((slots, units), F32),
            pltpu.VMEM((slots, LANES), F32),
            pltpu.VMEM((slots, LANES), F32),
        ],
        moved=4 * MIB,
    )
    sends, act, peak, top = call(
        lambda *refs: second_kernel(his, los, *refs),
        8,
        near(gain, wg, wu_first, wu_rest, wd, *sums, *helds),
        [
            pltpu.VMEM((los - 1, slots, his * cols + LANES), BF),
            pltpu.VMEM((slots, units), BF),
            pltpu.VMEM((SUBLANES, LANES), F32),
            pltpu.VMEM((SUBLANES, LANES), F32),
        ],
    )
    sends = [shift(sends[k - 1], "lo", k) for k in range(1, los)]
    (keep,) = call(
        lambda *refs: third_kernel(his, los, *refs),
        8,
        near(act, wd),
        [pltpu.VMEM((slots, his * cols), F32)],
        moved=2 * MIB,
    )
    (back,) = call(
        lambda *refs: pair_kernel(his, los - 1, *refs),
        4,
        near(keep, peak, *sends),
        [pltpu.VMEM((blocks, EXPERT_SLOTS, cols + LANES), BF)],
    )
    back = lax.all_to_all(back, ("dp", "hi"), 0, 0, tiled=True)
    (tile,) = call(
        lambda *refs: hold_kernel(his, *refs),
        1,
        near(back),
        [pltpu.VMEM((EXPERT_SLOTS, LANES), F32)],
    )
    layer_out, input_top, hidden_top = pl.pallas_call(
        lambda *refs: combine_kernel(his, *refs),
        out_shape=[
            jax.ShapeDtypeStruct((tokens, cols), BF),
            jax.ShapeDtypeStruct((1,), F32),
            jax.ShapeDtypeStruct((1,), F32),
        ],
        in_specs=[VMEM] * (4 + his),
        out_specs=[VMEM, SMEM, SMEM],
        compiler_params=pltpu.CompilerParams(vmem_limit_bytes=4 * MIB),
        name="combine",
    )(mine, comb, back, top, tile, *rests)
    return layer_out, input_top, hidden_top


def solution(mesh):
    tp = mesh.shape["tp"]
    lo = 2 if tp % 2 == 0 else 1
    split = Mesh(mesh.devices.reshape(mesh.shape["dp"], tp // lo, lo), ("dp", "hi", "lo"))
    tps = ("hi", "lo")
    placed = (
        P(tps, "dp", None),
        P("dp", tps),
        P(),
        P("dp", None),
        P("dp", None),
        P("dp", None, tps),
        P("dp", None, tps),
        P("dp", tps, None),
    )

    return jax.shard_map(
        on_device,
        mesh=split,
        in_specs=placed,
        out_specs=(P("dp", tps), P("dp"), P("dp")),
        check_vma=False,
    )
```
